256 devices in a mesh: ctx: 32 (over z_hi, y, core), rep: 8 (over z_lo, x).
Axes of the slice: x: 4, y: 4, z: 8 (z_hi: 4, z_lo: 2; z = z_hi * 2 + z_lo), core: 2. Of those that a mesh axis runs over, the one named last changes fastest.
Arguments:
- tokens: bfloat16 [8192, 8192], P('ctx'), may hold values from -6 to 6
- norm_gain: bfloat16 [8192], replicated, may hold values from 0.099609375 to 1.8984375
- q_weight: bfloat16 [8192, 4096], P('ctx', 'rep'), may hold values from -0.0625 to 0.0625
- q_bias: bfloat16 [4096], P('rep'), may hold values from -48 to 48
- key_value_weight: bfloat16 [8192, 1024], P('ctx', 'rep'), may hold values from -0.0625 to 0.0625
- kv_bias: bfloat16 [1024], P('rep'), may hold values from -8 to 8
- out_weight: bfloat16 [4096, 8192], P('rep', 'ctx'), may hold values from -0.5 to 0.5
Outputs:
- attn_out: bfloat16 [8192, 8192], P(('ctx', 'rep'))
- key_value_cache: bfloat16 [8192, 1024], P('ctx')
The draws below stay inside these ranges and needn't reach their ends.
All inputs are finite; a program needn't handle non-finite values.
Results may differ from the reference program's by a relative error of at most 0.014.
The reference program's roundings to bfloat16 on the way count: a program that leaves them out, or rounds other values in their place, can miss the bound.
Values may be sent and summed in bfloat16 or wider, within the bound.
A program may use at most 128 MiB of HBM per device.

```python
import jax
import jax.numpy as jnp
from jax import lax

MODEL_WIDTH = 8192
HEAD_SIZE = 128
QUERY_HEADS = 32
KEY_VALUE_HEADS = 4
PREFIX_TOKENS = 8192
N_REP = 8


def bias_parts(key):
    key_offset_bias = jax.random.normal(jax.random.fold_in(key, 11), (KEY_VALUE_HEADS, HEAD_SIZE), jnp.float32)
    value_offset_bias = 0.5 * jax.random.normal(jax.random.fold_in(key, 12), (KEY_VALUE_HEADS * HEAD_SIZE,), jnp.float32)
    random_jitter = jax.random.normal(jax.random.fold_in(key, 14), (QUERY_HEADS, HEAD_SIZE), jnp.float32)
    key_offset_bias = 0.5 * key_offset_bias
    query_offset_bias = 0.5 * random_jitter
    return (query_offset_bias.reshape(-1), jnp.concatenate([key_offset_bias.reshape(-1), value_offset_bias]))


def draw_q_bias(key, part):
    query_offset_bias, other = bias_parts(key)
    return jnp.clip(query_offset_bias, -48.0, 48.0).astype(jnp.bfloat16)


def draw_kv_bias(key, part):
    other, kv_part = bias_parts(key)
    return jnp.clip(kv_part, -8.0, 8.0).astype(jnp.bfloat16)


def level_of(stream_key, extent, cuts, least, top_value):
    gain = 1.0
    for position, blocks in cuts:
        draws = jax.random.uniform(jax.random.fold_in(jax.random.fold_in(stream_key, 6), position), (blocks,), jnp.float32, least / len(cuts), top_value / len(cuts))
        gain = gain * jnp.repeat(jnp.exp(draws), extent[position] // blocks).reshape((-1,) + (1,) * (len(extent) - 1 - position))
    return gain


def normal_values(key, dims, spread, limit, cuts=(), held_as=jnp.bfloat16):
    factor_of = level_of(key, dims, cuts, -0.22, 0.18) if cuts else 1.0
    drawn = jax.random.normal(key, dims, jnp.float32) * spread * factor_of
    return jnp.minimum(jnp.maximum(drawn, -limit), limit).astype(held_as)


def setup_inputs(seed: int = 0) -> dict:
    key_of = jax.random.split(jax.random.key(seed), 8)
    return {
        "tokens": normal_values(key_of[0], (PREFIX_TOKENS, MODEL_WIDTH), 1.0, 6.0, ((0, 32),)),
        "norm_gain": jnp.clip(1.0 + 0.18 * jax.random.normal(key_of[1], (MODEL_WIDTH,), jnp.float32), 0.099609375, 1.8984375).astype(jnp.bfloat16),
        "q_weight": normal_values(key_of[2], (MODEL_WIDTH, QUERY_HEADS * HEAD_SIZE), MODEL_WIDTH ** -0.5, 0.0625, ((0, 32), (1, 8))),
        "q_bias": draw_q_bias(jax.random.fold_in(key_of[7], 71), 0),
        "key_value_weight": normal_values(key_of[4], (MODEL_WIDTH, 2 * KEY_VALUE_HEADS * HEAD_SIZE), MODEL_WIDTH ** -0.5, 0.0625, ((0, 32), (1, 8))),
        "kv_bias": draw_kv_bias(jax.random.fold_in(key_of[7], 71), 0),
        "out_weight": normal_values(key_of[6], (QUERY_HEADS * HEAD_SIZE, MODEL_WIDTH), HEAD_SIZE ** -0.5, 0.5, ((0, 8), (1, 32))),
    }


rope_base = 1000000.0

def apply_rotation(value_rows, token_positions):
    middle = value_rows.shape[-1] // 2
    exponent = jnp.arange(middle, dtype=jnp.float32) * (2.0 / value_rows.shape[-1])
    inverse = rope_base ** (-exponent)
    angles = token_positions.astype(jnp.float32)[:, None] * inverse[None, :]
    cosine = jnp.cos(angles)[:, None, :]
    sine_part = jnp.sin(angles)[:, None, :]
    leading = value_rows[..., :middle]
    trailing = value_rows[..., middle:]
    return jnp.concatenate([leading * cosine - trailing * sine_part, trailing * cosine + leading * sine_part], axis=-1)

def reference(tokens, norm_gain, q_weight, q_bias, key_value_weight, kv_bias, out_weight):
    values_in = tokens.astype(jnp.float32)
    scale_row = lax.rsqrt(lax.optimization_barrier(jnp.mean(values_in * values_in, axis=-1, keepdims=True)) + 1e-06)
    normed = (values_in * scale_row * norm_gain.astype(jnp.float32)).astype(jnp.bfloat16)
    token_positions = jnp.arange(PREFIX_TOKENS, dtype=jnp.int32)
    query_sum = jnp.dot(normed, q_weight, preferred_element_type=jnp.float32) + q_bias.astype(jnp.float32)
    query_rows = apply_rotation(query_sum.reshape(PREFIX_TOKENS, QUERY_HEADS, HEAD_SIZE), token_positions).astype(jnp.bfloat16)
    key_value_sum = jnp.dot(normed, key_value_weight, preferred_element_type=jnp.float32) + kv_bias.astype(jnp.float32)
    key_section = apply_rotation(key_value_sum[:, :KEY_VALUE_HEADS * HEAD_SIZE].reshape(PREFIX_TOKENS, KEY_VALUE_HEADS, HEAD_SIZE), token_positions).reshape(PREFIX_TOKENS, KEY_VALUE_HEADS * HEAD_SIZE)
    key_value_cache = jnp.concatenate([key_section, key_value_sum[:, KEY_VALUE_HEADS * HEAD_SIZE:]], axis=1).astype(jnp.bfloat16)
    key_rows = key_value_cache[:, :KEY_VALUE_HEADS * HEAD_SIZE].reshape(PREFIX_TOKENS, KEY_VALUE_HEADS, HEAD_SIZE).astype(jnp.float32)
    value_rows = key_value_cache[:, KEY_VALUE_HEADS * HEAD_SIZE:].reshape(PREFIX_TOKENS, KEY_VALUE_HEADS, HEAD_SIZE).astype(jnp.float32)
    head_group = QUERY_HEADS // KEY_VALUE_HEADS
    grouped_rows = query_rows.reshape(PREFIX_TOKENS, KEY_VALUE_HEADS, head_group, HEAD_SIZE).astype(jnp.float32)
    block = min(512, PREFIX_TOKENS)
    pieces = []
    for index in range(PREFIX_TOKENS // block):
        finish = (index + 1) * block
        query_block = grouped_rows[index * block:finish]
        scores = jnp.einsum('rgjd,pgd->gjrp', query_block, key_rows[:finish]) * HEAD_SIZE ** (-0.5)
        query_pos = jnp.arange(index * block, finish, dtype=jnp.int32)
        key_pos = jnp.arange(finish, dtype=jnp.int32)
        allowed = key_pos[None, :] <= query_pos[:, None]
        scores = jnp.where(allowed, scores, -1e+30)
        maximum = lax.optimization_barrier(jnp.max(scores, axis=-1, keepdims=True))
        expo = jnp.where(allowed, jnp.exp(scores - maximum), 0.0)
        total = lax.optimization_barrier(jnp.sum(expo, axis=-1))
        weights = expo.astype(jnp.bfloat16).astype(jnp.float32)
        summed = jnp.einsum('gjrp,pgd->gjrd', weights, value_rows[:finish])
        result = summed / total[..., None]
        pieces.append(jnp.transpose(result, (2, 0, 1, 3)).reshape(block, QUERY_HEADS * HEAD_SIZE).astype(jnp.bfloat16))
    attended = jnp.concatenate(pieces, axis=0)
    width = QUERY_HEADS * HEAD_SIZE // N_REP
    accum = jnp.zeros((PREFIX_TOKENS, MODEL_WIDTH), jnp.float32)
    for member in range(N_REP):
        partial_value = jnp.dot(attended[:, member * width:(member + 1) * width], out_weight[member * width:(member + 1) * width], preferred_element_type=jnp.float32)
        rounded = lax.optimization_barrier(partial_value.astype(jnp.bfloat16))
        accum = accum + rounded.astype(jnp.float32)
    return (accum.astype(jnp.bfloat16), key_value_cache)
```

```python
import functools

import jax
import jax.numpy as jnp
from jax import lax
from jax.experimental import pallas as pl
from jax.experimental.pallas import tpu as pltpu
from jax.sharding import PartitionSpec as P

MESH = pl.DeviceIdType.MESH
F32 = jnp.float32
BF16 = jnp.bfloat16

HEAD = 128
Q_HEADS = 32
KV_HEADS = 4
ROWS = 256
WIDTH = 8192
CTX = 32
REP = 8
LOCAL = Q_HEADS // REP
ROPE_BASE = 1000000.0
EXP_SCALE = HEAD ** (-0.5) * 1.4426950408889634
NEG = -1e30


def ctx_of(zh, y, k):
    return zh * 8 + y * 2 + k


def send(src, dst, send_sem, recv_sem, device):
    pltpu.make_async_remote_copy(
        src_ref=src,
        dst_ref=dst,
        send_sem=send_sem,
        recv_sem=recv_sem,
        device_id=device,
        device_id_type=MESH,
    ).start()


def wait(ref, sem):
    pltpu.make_async_copy(ref, ref, sem).wait()


def rotate(v, cos, sin):
    return v * cos + pltpu.roll(v, HEAD // 2, 1) * sin


def gather_steps(buf, own, halves, z_first, where, send_sem, recv_sem):
    zh, y, k, r = where
    a, b = (zh, y) if z_first else (y, zh)

    def slot(a_, b_, k_=k):
        return ctx_of(a_, b_, k_) if z_first else ctx_of(b_, a_, k_)

    def device(da, db):
        return (slot(lax.rem(a + da, 4), lax.rem(b + db, 4)), r)

    partner = (slot(a, b, 1 - k), r)
    rows = (a, lax.rem(a + 3, 4), lax.rem(a + 1, 4), lax.rem(a + 2, 4))
    before, after, across = lax.rem(b + 3, 4), lax.rem(b + 1, 4), lax.rem(b + 2, 4)

    def full(s, sem, dev, src=None):
        send(buf.at[s] if src is None else src, buf.at[s], send_sem, recv_sem.at[sem], dev)

    def half(s, which, sem, dev):
        send(halves(s, which), halves(s, which), send_sem, recv_sem.at[sem], dev)

    def arrived(s, sem):
        wait(buf.at[s], recv_sem.at[sem])

    def spread(row, src=None):
        s = slot(rows[row], b)
        full(s, 3 + 3 * row, device(0, 1), src)
        full(s, 4 + 3 * row, device(0, 3), src)
        full(s, 15 + row, partner, src)

    def start():
        s = slot(a, b)
        full(s, 0, device(1, 0), own)
        full(s, 1, device(3, 0), own)
        spread(0, own)

    def first_before():
        s = slot(rows[1], b)
        arrived(s, 0)
        half(s, 0, 2, device(1, 0))
        spread(1)

    def first_after():
        s = slot(rows[2], b)
        arrived(s, 1)
        half(s, 1, 2, device(3, 0))
        spread(2)

    def first_across():
        arrived(slot(rows[3], b), 2)
        spread(3)

    def second(row):
        def step():
            s = slot(rows[row], before)
            arrived(s, 3 + 3 * row)
            half(s, 0, 5 + 3 * row, device(0, 1))
            full(s, 15 + row, partner)
            s = slot(rows[row], after)
            arrived(s, 4 + 3 * row)
            half(s, 1, 5 + 3 * row, device(0, 3))
            full(s, 15 + row, partner)

        return step

    def second_across(row):
        def step():
            s = slot(rows[row], across)
            arrived(s, 5 + 3 * row)
            full(s, 15 + row, partner)

        return step

    steps = {
        "start": start,
        "a": first_before,
        "b": first_after,
        "c": first_across,
        "r0": second(0),
        "r1": second(1),
        "r2": second(2),
        "r3": second(3),
        "x0": second_across(0),
        "x1": second_across(1),
        "x2": second_across(2),
        "x3": second_across(3),
    }

    def row_done(row):
        wait(buf.at[pl.ds(0, 4)], recv_sem.at[15 + row])

    def sent():
        wait(buf.at[pl.ds(0, 31)], send_sem)

    return steps, rows, row_done, sent


def kernel(
    tok_hbm,
    qw_hbm,
    kvw_hbm,
    ow_hbm,
    gain_ref,
    cos_ref,
    sin_ref,
    qb_ref,
    kvb_ref,
    out_ref,
    cache_ref,
    tok,
    qw,
    kvw,
    kv,
    ow,
    att,
    outp,
    qs,
    acc,
    kvacc,
    m_ref,
    l_ref,
    o_ref,
    local_sem,
    ag_send,
    kvw_recv,
    qw_recv,
    kv_recv,
    cache_send,
    cache_recv,
    ow_send,
    ow_z,
    ow_y,
    ow_p,
    att_send,
    att_z,
    att_x,
    a2a_send,
    a2a_recv,
):
    c = lax.axis_index("ctx")
    r = lax.axis_index("rep")
    k = lax.rem(c, 2)
    y = lax.rem(lax.div(c, 2), 4)
    zh = lax.div(c, 8)
    x = lax.rem(r, 4)
    zl = lax.div(r, 4)
    where = (zh, y, k, r)
    c_pair = c - k

    def rep_peer(i):
        return lax.rem(r + i, REP)

    tok_copy = pltpu.make_async_copy(tok_hbm, tok, local_sem.at[0])
    tok_copy.start()
    kvw_own = pltpu.make_async_copy(kvw_hbm, kvw.at[c], local_sem.at[1])
    kvw_own.start()
    qw_own = pltpu.make_async_copy(qw_hbm, qw.at[c], local_sem.at[2])
    qw_own.start()

    barrier = pltpu.get_barrier_semaphore()
    greet = [(c_pair + k, rep_peer(i)) for i in range(1, REP)]
    greet += [(c_pair + 1 - k, rep_peer(i)) for i in range(REP)]
    greet += [(ctx_of(zh, lax.rem(y + d, 4), k), r) for d in (1, 3)]
    greet += [(ctx_of(lax.rem(zh + d, 4), y, k), r) for d in (1, 3)]
    for dev in greet:
        pl.semaphore_signal(barrier, inc=1, device_id=dev, device_id_type=MESH)
    pl.semaphore_wait(barrier, len(greet))

    kvw_steps, kvw_rows, kvw_row_done, kvw_sent = gather_steps(
        kvw, kvw_hbm, lambda s, i: kvw.at[s, pl.ds(128 * i, 128)], True, where, ag_send.at[0], kvw_recv
    )
    q_steps, q_rows, q_row_done, q_sent = gather_steps(
        qw, qw_hbm, lambda s, i: qw.at[s, pl.ds(128 * i, 128)], True, where, ag_send.at[1], qw_recv
    )
    kv_steps, kv_rows, kv_row_done, kv_sent = gather_steps(
        kv, None, lambda s, i: kv.at[s, i], True, where, ag_send.at[2], kv_recv
    )

    collector = 2 * zh + k
    at_home = (r == collector) & (zl == k)
    ow_mine = y * 8 + r
    ow_local = pltpu.make_async_copy(ow_hbm, ow.at[ow_mine], ow_z.at[x])

    def ow_collect():
        @pl.when(at_home)
        def _():
            ow_local.start()

        @pl.when(jnp.logical_not(at_home))
        def _():
            send(ow_hbm, ow.at[ow_mine], ow_send.at[0], ow_z.at[x], (ctx_of(zh, y, zl), collector))

    away = lax.rem(zh - lax.div(r, 2) + 4, 4)
    z_next = (ctx_of(lax.rem(zh + 1, 4), y, k), r)
    z_last = (ctx_of(lax.rem(zh + 3, 4), y, k), r)
    y_next = (ctx_of(zh, lax.rem(y + 1, 4), k), r)
    y_last = (ctx_of(zh, lax.rem(y + 3, 4), k), r)
    partner = (ctx_of(zh, y, 1 - k), r)
    y_rows = (y, lax.rem(y + 3, 4), lax.rem(y + 1, 4), lax.rem(y + 2, 4))

    def ow_half(s, i):
        return ow.at[s, pl.ds(256 * i, 256)]

    def ow_a(i):
        s = y * 8 + 4 * k + i
        wait(ow.at[s], ow_z.at[i])

        @pl.when(away == 0)
        def _():
            send(ow.at[s], ow.at[s], ow_send.at[1], ow_z.at[i], z_next)
            send(ow.at[s], ow.at[s], ow_send.at[1], ow_z.at[i], z_last)

        @pl.when(away == 1)
        def _():
            send(ow_half(s, 0), ow_half(s, 0), ow_send.at[1], ow_z.at[i], z_next)

        @pl.when(away == 3)
        def _():
            send(ow_half(s, 1), ow_half(s, 1), ow_send.at[1], ow_z.at[i], z_last)

        send(ow.at[s], ow.at[s], ow_send.at[2], ow_y.at[i, 0], y_next)
        send(ow.at[s], ow.at[s], ow_send.at[2], ow_y.at[i, 1], y_last)
        send(ow.at[s], ow.at[s], ow_send.at[2], ow_p.at[0], partner)

    def ow_b(i):
        s = y_rows[1] * 8 + 4 * k + i
        wait(ow.at[s], ow_y.at[i, 0])
        send(ow_half(s, 0), ow_half(s, 0), ow_send.at[2], ow_y.at[i, 2], y_next)
        send(ow.at[s], ow.at[s], ow_send.at[2], ow_p.at[1], partner)
        s = y_rows[2] * 8 + 4 * k + i
        wait(ow.at[s], ow_y.at[i, 1])
        send(ow_half(s, 1), ow_half(s, 1), ow_send.at[2], ow_y.at[i, 2], y_last)
        send(ow.at[s], ow.at[s], ow_send.at[2], ow_p.at[2], partner)

    def ow_c(i):
        s = y_rows[3] * 8 + 4 * k + i
        wait(ow.at[s], ow_y.at[i, 2])
        send(ow.at[s], ow.at[s], ow_send.at[2], ow_p.at[3], partner)

    def ow_row_done(row):
        wait(ow.at[pl.ds(0, 4)], ow_p.at[row])

    def ow_sent():
        @pl.when(jnp.logical_not(at_home))
        def _():
            wait(ow.at[0], ow_send.at[0])

        @pl.when(away == 0)
        def _():
            wait(ow.at[pl.ds(0, 8)], ow_send.at[1])

        @pl.when((away == 1) | (away == 3))
        def _():
            wait(ow.at[pl.ds(0, 2)], ow_send.at[1])

        wait(ow.at[pl.ds(0, 28)], ow_send.at[2])

    kvw_steps["start"]()
    ow_collect()
    tok_copy.wait()

    def normalize(i, carry):
        rows = pl.ds(pl.multiple_of(i * 32, 32), 32)
        squares = jnp.zeros((32, 128), F32)
        for j in range(WIDTH // 128):
            v = tok[rows, j * 128 : (j + 1) * 128].astype(F32)
            squares = squares + v * v
        mean = jnp.sum(squares, axis=-1, keepdims=True) * (1.0 / WIDTH)
        scale = lax.rsqrt(mean + 1e-06)
        for j in range(WIDTH // 128):
            cols = slice(j * 128, (j + 1) * 128)
            v = tok[rows, cols].astype(F32)
            tok[rows, cols] = (v * scale * gain_ref[:, cols].astype(F32)).astype(BF16)
        return carry

    lax.fori_loop(0, 4, normalize, 0)
    for name in ("a", "b", "r0"):
        kvw_steps[name]()
    lax.fori_loop(4, 8, normalize, 0)
    for name in ("c", "r1", "r2", "x0"):
        kvw_steps[name]()
    q_steps["start"]()
    for name in ("r3", "x1", "x2", "x3"):
        kvw_steps[name]()

    kvw_own.wait()
    for row in range(4):
        kvw_row_done(row)

    kvacc[...] = jnp.zeros_like(kvacc)

    def kv_product(i, carry):
        cols = pl.ds(pl.multiple_of(i * 512, 512), 512)
        kvacc[...] += jnp.dot(
            tok[:, cols], kvw[pl.ds(2 * i, 2)].reshape(512, HEAD), preferred_element_type=F32
        )
        return carry

    lax.fori_loop(0, 16, kv_product, 0)
    plain = kvacc[...] + kvb_ref[...].astype(F32)
    is_key = r < KV_HEADS
    mine = jnp.where(is_key, rotate(plain, cos_ref[...], sin_ref[...]), plain).astype(BF16)
    my_block = cache_ref.at[:, pl.ds(pl.multiple_of(r * HEAD, HEAD), HEAD)]
    my_block[...] = mine
    for i in range(1, REP):
        send(my_block, my_block, cache_send, cache_recv, (c, rep_peer(i)))

    for name in ("a", "b", "r0"):
        q_steps[name]()

    wait(kv.at[pl.ds(0, 7), 0], cache_recv)
    kv_head = lax.div(r, 2)
    for i in range(2):
        block = cache_ref.at[:, pl.ds(pl.multiple_of((i * KV_HEADS + kv_head) * HEAD, HEAD), HEAD)]
        copy = pltpu.make_async_copy(block, kv.at[c, i], local_sem.at[3 + i])
        copy.start()
        copy.wait()
    kv_steps["start"]()

    for name in ("c", "r1", "r2"):
        q_steps[name]()
    for name in ("a", "b", "r0"):
        kv_steps[name]()

    acc[...] = jnp.zeros_like(acc)
    qw_own.wait()

    def q_group(row):
        base = q_rows[row]

        def q_product(i, carry):
            cols = pl.ds(pl.multiple_of(base * 2048 + i * 512, 512), 512)
            acc[...] += jnp.dot(
                tok[:, cols],
                qw[pl.ds(base * 8 + 2 * i, 2)].reshape(512, LOCAL * HEAD),
                preferred_element_type=F32,
            )
            return carry

        q_row_done(row)
        lax.fori_loop(0, 4, q_product, 0)

    q_steps["x0"]()
    q_steps["r3"]()
    for name in ("c", "r1", "r2"):
        kv_steps[name]()
    for i in range(4):
        ow_a(i)
    q_group(0)
    q_steps["x1"]()
    q_group(1)
    q_steps["x2"]()
    kv_steps["x0"]()
    kv_steps["r3"]()
    q_group(2)
    q_steps["x3"]()
    for name in ("x1", "x2"):
        kv_steps[name]()
    ow_b(0)
    q_group(3)
    kv_steps["x3"]()

    for h in range(LOCAL):
        cols = slice(h * HEAD, (h + 1) * HEAD)
        v = acc[:, cols] + qb_ref[:, cols].astype(F32)
        qs[h] = rotate(v, cos_ref[...], sin_ref[...]).astype(BF16)
    for row in range(4):
        kv_row_done(row)

    last = lax.div(c, 2)

    def attend(h):
        m_ref[...] = jnp.full_like(m_ref, NEG)
        l_ref[...] = jnp.zeros_like(l_ref)
        o_ref[...] = jnp.zeros_like(o_ref)

        def block(j, masked):
            keys = kv[pl.ds(2 * j, 2), 0].reshape(512, HEAD)
            values = kv[pl.ds(2 * j, 2), 1].reshape(512, HEAD)
            s = lax.dot_general(
                qs[h], keys, (((1,), (1,)), ((), ())), preferred_element_type=F32
            )
            if masked:
                key_pos = j * 512 + lax.broadcasted_iota(jnp.int32, s.shape, 1)
                query_pos = c * ROWS + lax.broadcasted_iota(jnp.int32, s.shape, 0)
                s = jnp.where(key_pos <= query_pos, s, NEG)
            m_old = m_ref[...]
            m_new = jnp.maximum(m_old, jnp.max(s, axis=-1, keepdims=True))
            p = jnp.exp2((s - m_new[:, :1]) * EXP_SCALE)
            alpha = jnp.exp2((m_old - m_new) * EXP_SCALE)
            l_ref[...] = l_ref[...] * alpha + jnp.sum(p, axis=-1, keepdims=True)
            o_ref[...] = o_ref[...] * alpha + jnp.dot(
                p.astype(BF16), values, preferred_element_type=F32
            )
            m_ref[...] = m_new

        def step(j, carry):
            block(j, False)
            return carry

        lax.fori_loop(0, last, step, 0)
        block(last, True)
        part = att.at[r, :, pl.ds(h * HEAD, HEAD)]
        part[...] = (o_ref[...] / l_ref[...]).astype(BF16)
        send(part, part, att_send, att_z.at[h], (c, lax.rem(r + 4, REP)))
        for i in range(1, 4):
            send(part, part, att_send, att_x.at[h], (c, zl * 4 + lax.rem(x + i, 4)))

    def att_forward(h):
        part = att.at[lax.rem(r + 4, REP), :, pl.ds(h * HEAD, HEAD)]
        wait(part, att_z.at[h])
        for i in range(1, 4):
            send(part, part, att_send, att_x.at[h], (c, zl * 4 + lax.rem(x + i, 4)))

    attend(0)
    ow_b(1)
    attend(1)
    att_forward(0)
    ow_b(2)
    ow_c(0)
    attend(2)
    att_forward(1)
    ow_b(3)
    ow_c(1)
    attend(3)
    att_forward(2)
    ow_c(2)
    att_forward(3)
    ow_c(3)
    for h in range(LOCAL):
        wait(att.at[pl.ds(0, 6), :, pl.ds(h * HEAD, HEAD)], att_x.at[h])

    zs = lax.div(r, 2)
    ks = lax.rem(r, 2)
    for row in range(4):
        ow_row_done(row)
        acc[:, :ROWS] = jnp.zeros((ROWS, 256), F32)

        def o_product(g, carry):
            part = jnp.dot(att[g], ow[y_rows[row] * 8 + g], preferred_element_type=F32)
            acc[:, :ROWS] += part.astype(BF16).astype(F32)
            return carry

        lax.fori_loop(0, REP, o_product, 0)
        outp[row] = acc[:, :ROWS].astype(BF16)
        column = pl.multiple_of(ctx_of(zs, y_rows[row], ks) * 256, 256)
        dst = out_ref.at[:, pl.ds(column, 256)]
        for i in range(1, REP):
            peer = rep_peer(i)
            src = outp.at[row, pl.ds(pl.multiple_of(peer * 32, 32), 32)]
            send(src, dst, a2a_send, a2a_recv.at[row], (c, peer))
        dst[...] = outp[row, pl.ds(pl.multiple_of(r * 32, 32), 32), :]

    for row in range(4):
        wait(outp.at[0, pl.ds(0, 224)], a2a_recv.at[row])

    kvw_sent()
    q_sent()
    kv_sent()
    ow_sent()
    wait(kv.at[pl.ds(0, 7), 0], cache_send)
    wait(att.at[pl.ds(0, 7)], att_send)
    wait(kv.at[pl.ds(0, 7), 0], a2a_send)


def per_device(tokens, norm_gain, q_weight, q_bias, key_value_weight, kv_bias, out_weight):
    positions = lax.axis_index("ctx") * ROWS + jnp.arange(ROWS, dtype=jnp.int32)
    half = HEAD // 2
    exponent = jnp.arange(half, dtype=F32) * (2.0 / HEAD)
    inverse = ROPE_BASE ** (-exponent)
    angles = positions.astype(F32)[:, None] * inverse[None, :]
    cosine, sine = jnp.cos(angles), jnp.sin(angles)
    cos = jnp.concatenate([cosine, cosine], axis=-1)
    sin = jnp.concatenate([-sine, sine], axis=-1)
    any_spec = pl.BlockSpec(memory_space=pl.ANY)
    vmem_spec = pl.BlockSpec(memory_space=pltpu.VMEM)
    dma = pltpu.SemaphoreType.DMA
    return pl.pallas_call(
        kernel,
        out_shape=(
            jax.ShapeDtypeStruct((ROWS // REP, WIDTH), BF16),
            jax.ShapeDtypeStruct((ROWS, 2 * KV_HEADS * HEAD), BF16),
        ),
        in_specs=[any_spec] * 4 + [vmem_spec] * 5,
        out_specs=(vmem_spec, vmem_spec),
        scratch_shapes=[
            pltpu.VMEM((ROWS, WIDTH), BF16),
            pltpu.VMEM((CTX, 256, LOCAL * HEAD), BF16),
            pltpu.VMEM((CTX, 256, HEAD), BF16),
            pltpu.VMEM((CTX, 2, ROWS, HEAD), BF16),
            pltpu.VMEM((CTX, LOCAL * HEAD, 256), BF16),
            pltpu.VMEM((REP, ROWS, LOCAL * HEAD), BF16),
            pltpu.VMEM((4, ROWS, 256), BF16),
            pltpu.VMEM((LOCAL, ROWS, HEAD), BF16),
            pltpu.VMEM((ROWS, LOCAL * HEAD), F32),
            pltpu.VMEM((ROWS, HEAD), F32),
            pltpu.VMEM((ROWS, HEAD), F32),
            pltpu.VMEM((ROWS, HEAD), F32),
            pltpu.VMEM((ROWS, HEAD), F32),
            dma((5,)),
            dma((3,)),
            dma((19,)),
            dma((19,)),
            dma((19,)),
            dma,
            dma,
            dma((3,)),
            dma((4,)),
            dma((4, 3)),
            dma((4,)),
            dma,
            dma((4,)),
            dma((4,)),
            dma,
            dma((4,)),
        ],
        compiler_params=pltpu.CompilerParams(
            collective_id=0, has_side_effects=True, vmem_limit_bytes=60 << 20
        ),
    )(
        tokens,
        q_weight,
        key_value_weight,
        out_weight,
        norm_gain.reshape(1, WIDTH),
        cos,
        sin,
        q_bias.reshape(1, LOCAL * HEAD),
        kv_bias.reshape(1, HEAD),
    )


def solution(mesh):
    in_specs = (
        P("ctx", None),
        P(),
        P("ctx", "rep"),
        P("rep"),
        P("ctx", "rep"),
        P("rep"),
        P("rep", "ctx"),
    )
    out_specs = (P(("ctx", "rep"), None), P("ctx", None))
    return jax.shard_map(
        per_device, mesh=mesh, in_specs=in_specs, out_specs=out_specs, check_vma=False
    )
```

```python
import functools

import jax
import jax.numpy as jnp
from jax import lax
from jax.experimental import pallas as pl
from jax.experimental.pallas import tpu as pltpu
from jax.sharding import PartitionSpec as P

MESH = pl.DeviceIdType.MESH
F32 = jnp.float32
BF16 = jnp.bfloat16

HEAD = 128
Q_HEADS = 32
KV_HEADS = 4
ROWS = 256
WIDTH = 8192
CTX = 32
REP = 8
LOCAL = Q_HEADS // REP
ROPE_BASE = 1000000.0
EXP_SCALE = HEAD ** (-0.5) * 1.4426950408889634
NEG = -1e30

ORDER = (
    "k_t", "k_s", "n0", "p_s", "q_t", "k_r0", "p_t", "n1", "k_x0", "k_b",
    "k_a", "q_r0", "q_s", "k_r2", "k_c", "k_r1", "n2", "n3", "p_r0", "kg0",
    "og0", "k_x2", "k_r3", "p_b", "ozs0", "k_x1", "k_x3", "q_b", "q_x0", "q_a",
    "kg2", "kg1", "p_x0", "kg3", "cs", "q_r2", "cw", "v_t", "v_s", "p_a",
    "qg0", "p_r2", "v_r0", "ozs1", "q_r1", "v_a", "p_r1", "v_x0", "v_b", "q_x2",
    "p_c", "q_x1", "p_x2", "q_c", "v_r1", "v_r2", "v_c", "p_x1", "oz2", "vr0",
    "oz1", "og1", "og2", "p_r3", "q_r3", "v_x2", "v_r3", "oy0", "p_x3", "q_x3",
    "qg2", "oz3", "v_x3", "vr2", "v_x1", "og3", "qg1", "oy1", "qg3", "qf",
    "cr", "at00", "vr3", "at20", "vr1", "oy2", "at01", "at30", "oy3", "ob1",
    "at10", "as1", "as0", "ob0", "at31", "at11", "at21", "as2", "as3", "ap1",
    "ob2", "ap0", "ap2", "ob3", "ox1", "ap3", "aw", "out0", "ox0", "out2",
    "ox2", "out1", "ox3", "out3",
)


def ctx_of(zh, y, k):
    return zh * 8 + y * 2 + k


def send(src, dst, send_sem, recv_sem, device):
    pltpu.make_async_remote_copy(
        src_ref=src,
        dst_ref=dst,
        send_sem=send_sem,
        recv_sem=recv_sem,
        device_id=device,
        device_id_type=MESH,
    ).start()


def wait(ref, sem):
    pltpu.make_async_copy(ref, ref, sem).wait()


def rotate(v, cos, sin):
    return v * cos + pltpu.roll(v, HEAD // 2, 1) * sin


def gather_steps(buf, own, halves, z_first, where, send_sem, recv_sem, beside=None, beside_send=None):
    zh, y, k, r = where
    a, b = (zh, y) if z_first else (y, zh)

    def slot(a_, b_, k_=k):
        return ctx_of(a_, b_, k_) if z_first else ctx_of(b_, a_, k_)

    def device(da, db):
        return (slot(lax.rem(a + da, 4), lax.rem(b + db, 4)), r)

    partner = (slot(a, b, 1 - k), r)
    rows = (a, lax.rem(a + 3, 4), lax.rem(a + 1, 4), lax.rem(a + 2, 4))
    before, after, across = lax.rem(b + 3, 4), lax.rem(b + 1, 4), lax.rem(b + 2, 4)

    def full(s, sem, dev, src=None):
        send(buf.at[s] if src is None else src, buf.at[s], send_sem, recv_sem.at[sem], dev)

    def half(s, which, sem, dev):
        send(halves(s, which), halves(s, which), send_sem, recv_sem.at[sem], dev)

    def arrived(s, sem):
        wait(buf.at[s], recv_sem.at[sem])

    def share(s, row, src=None):
        full(s, 15 + row, partner, src)
        if beside is not None:
            send(buf.at[s] if src is None else src, buf.at[s], beside_send, recv_sem.at[19 + row], beside)

    def spread(row, src=None):
        s = slot(rows[row], b)
        full(s, 3 + 3 * row, device(0, 1), src)
        full(s, 4 + 3 * row, device(0, 3), src)
        share(s, row, src)

    def start_first():
        s = slot(a, b)
        full(s, 0, device(1, 0), own)
        full(s, 1, device(3, 0), own)

    def start_second():
        spread(0, own)

    def first_before():
        s = slot(rows[1], b)
        arrived(s, 0)
        half(s, 0, 2, device(1, 0))
        spread(1)

    def first_after():
        s = slot(rows[2], b)
        arrived(s, 1)
        half(s, 1, 2, device(3, 0))
        spread(2)

    def first_across():
        arrived(slot(rows[3], b), 2)
        spread(3)

    def second(row):
        def step():
            s = slot(rows[row], before)
            arrived(s, 3 + 3 * row)
            half(s, 0, 5 + 3 * row, device(0, 1))
            share(s, row)
            s = slot(rows[row], after)
            arrived(s, 4 + 3 * row)
            half(s, 1, 5 + 3 * row, device(0, 3))
            share(s, row)

        return step

    def second_across(row):
        def step():
            s = slot(rows[row], across)
            arrived(s, 5 + 3 * row)
            share(s, row)

        return step

    steps = {
        "s": start_first,
        "t": start_second,
        "a": first_before,
        "b": first_after,
        "c": first_across,
        "r0": second(0),
        "r1": second(1),
        "r2": second(2),
        "r3": second(3),
        "x0": second_across(0),
        "x1": second_across(1),
        "x2": second_across(2),
        "x3": second_across(3),
    }

    def row_done(row):
        wait(buf.at[pl.ds(0, 4)], recv_sem.at[15 + row])

    def sent():
        wait(buf.at[pl.ds(0, 31)], send_sem)

    return steps, rows, row_done, sent


def kernel(
    tok_hbm,
    qw_hbm,
    kvw_hbm,
    ow_hbm,
    gain_ref,
    cos_ref,
    sin_ref,
    qb_ref,
    kvb_ref,
    part_ref,
    cache_ref,
    tok,
    qw,
    kvw,
    kv,
    ow,
    oz,
    att,
    outp,
    qs,
    acc,
    kvacc,
    s_ref,
    m_ref,
    l_ref,
    o_ref,
    local_sem,
    ag_send,
    kvw_recv,
    qw_recv,
    kv_recv,
    cache_send,
    cache_recv,
    ow_send,
    oz_recv,
    ow_z,
    ow_y,
    ow_p,
    att_send,
    att_x,
    a2a_send,
    a2a_recv,
):
    c = lax.axis_index("ctx")
    r = lax.axis_index("rep")
    k = lax.rem(c, 2)
    y = lax.rem(lax.div(c, 2), 4)
    zh = lax.div(c, 8)
    x = lax.rem(r, 4)
    zl = lax.div(r, 4)
    where = (zh, y, k, r)
    c_pair = c - k

    def rep_peer(i):
        return lax.rem(r + i, REP)

    tok_copy = pltpu.make_async_copy(tok_hbm, tok, local_sem.at[0])
    tok_copy.start()
    kvw_own = pltpu.make_async_copy(kvw_hbm, kvw.at[c], local_sem.at[1])
    kvw_own.start()
    qw_own = pltpu.make_async_copy(qw_hbm, qw.at[c], local_sem.at[2])
    qw_own.start()

    barrier = pltpu.get_barrier_semaphore()
    greet = [(c_pair + k, rep_peer(i)) for i in range(1, REP)]
    greet += [(c_pair + 1 - k, rep_peer(i)) for i in range(REP)]
    greet += [(ctx_of(zh, lax.rem(y + d, 4), k), r) for d in (1, 3)]
    greet += [(ctx_of(lax.rem(zh + d, 4), y, k), r) for d in (1, 3)]
    for dev in greet:
        pl.semaphore_signal(barrier, inc=1, device_id=dev, device_id_type=MESH)
    pl.semaphore_wait(barrier, len(greet))

    kvw_steps, kvw_rows, kvw_row_done, kvw_sent = gather_steps(
        kvw, kvw_hbm, lambda s, i: kvw.at[s, pl.ds(128 * i, 128)], True, where, ag_send.at[0], kvw_recv
    )
    q_parts = []
    for i in range(2):
        view = qw.at[:, pl.ds(128 * i, 128)]
        q_parts.append(
            gather_steps(
                view,
                qw_hbm.at[pl.ds(128 * i, 128)],
                lambda s, j, i=i: qw.at[s, pl.ds(128 * i + 64 * j, 64)],
                True,
                where,
                ag_send.at[1 + 4 * i],
                qw_recv.at[i],
            )
        )
    q_rows = q_parts[0][1]
    side = lax.rem(r, 2)
    beside = (c, r + 1 - 2 * side)
    kv_mine, kv_other = kv.at[side], kv.at[1 - side]
    kv_steps, kv_rows, kv_row_done, kv_sent = gather_steps(
        kv_mine,
        None,
        lambda s, i: kv_mine.at[s, pl.ds(128 * i, 128)],
        True,
        where,
        ag_send.at[2],
        kv_recv,
        beside,
        ag_send.at[4],
    )

    def kv_relay(row):
        wait(kv_other.at[pl.ds(0, 4)], kv_recv.at[19 + row])
        for i in range(4):
            s = ctx_of(kv_rows[row], i, k)
            send(
                kv_other.at[s],
                kv_other.at[s],
                ag_send.at[3],
                kv_recv.at[23 + row],
                (ctx_of(zh, y, 1 - k), r),
            )

    z_next = (ctx_of(lax.rem(zh + 1, 4), y, k), r)
    z_last = (ctx_of(lax.rem(zh + 3, 4), y, k), r)
    y_next = (ctx_of(zh, lax.rem(y + 1, 4), k), r)
    y_last = (ctx_of(zh, lax.rem(y + 3, 4), k), r)
    partner = (ctx_of(zh, y, 1 - k), r)
    y_rows = (y, lax.rem(y + 3, 4), lax.rem(y + 1, 4), lax.rem(y + 2, 4))
    z_rows = (zh, lax.rem(zh + 3, 4), lax.rem(zh + 1, 4), lax.rem(zh + 2, 4))
    keeps = lax.rem(x, 2) == k

    def ow_place(y_, z_, first, count):
        cols = pl.ds(pl.multiple_of(128 * lax.rem(z_, 2), 128), 128)
        return ow.at[pl.ds(y_ * 8 + lax.div(z_, 2) * 4 + first, count), :, cols]

    def ow_pair(y_row, row):
        return ow_place(y_rows[y_row], z_rows[row], 2 * k, 2)

    def ow_half(y_row, row, i):
        return ow_place(y_rows[y_row], z_rows[row], 2 * k + i, 1)

    def oz_half(s, i):
        return oz.at[s, pl.ds(256 * i, 256)]

    def oz_start(i):
        rows = pl.ds(256 * i, 256)
        send(ow_hbm.at[rows], oz.at[zh, rows], ow_send.at[1], oz_recv.at[0], z_next)
        send(ow_hbm.at[rows], oz.at[zh, rows], ow_send.at[1], oz_recv.at[1], z_last)

    def oz_wait(row):
        s = z_rows[row]
        wait(oz.at[s], oz_recv.at[row - 1])
        if row == 1:
            send(oz_half(s, 0), oz_half(s, 0), ow_send.at[1], oz_recv.at[2], z_next)
        if row == 2:
            send(oz_half(s, 1), oz_half(s, 1), ow_send.at[1], oz_recv.at[2], z_last)

    def oz_give(row):
        z_ = z_rows[row]
        src = ow_hbm if row == 0 else oz.at[z_]
        spot = y * 8 + lax.div(z_, 2) * 4 + 2 * lax.rem(x, 2) + lax.div(x, 2)
        dst = ow.at[spot, :, pl.ds(pl.multiple_of(128 * lax.rem(z_, 2), 128), 128)]
        for j in range(2):
            worker = lax.rem(2 * k + j + z_, 4)
            part = src.at[:, pl.ds(128 * j, 128)]
            here = (worker == x) & keeps

            @pl.when(here)
            def _(part=part):
                pltpu.make_async_copy(part, dst, ow_z.at[row]).start()

            @pl.when(jnp.logical_not(here))
            def _(part=part, worker=worker):
                device = (ctx_of(zh, y, lax.rem(x, 2)), zl * 4 + worker)
                send(part, dst, ow_send.at[0], ow_z.at[row], device)

    def ow_y_start(i):
        part = ow_pair(0, i)
        wait(part, ow_z.at[i])
        send(part, part, ow_send.at[2], ow_y.at[i, 0], y_next)
        send(part, part, ow_send.at[2], ow_y.at[i, 1], y_last)
        send(part, part, ow_send.at[2], ow_p.at[0], partner)

    def ow_b(i):
        part, half = ow_pair(1, i), ow_half(1, i, 0)
        wait(part, ow_y.at[i, 0])
        send(half, half, ow_send.at[2], ow_y.at[i, 2], y_next)
        send(part, part, ow_send.at[2], ow_p.at[1], partner)
        part, half = ow_pair(2, i), ow_half(2, i, 1)
        wait(part, ow_y.at[i, 1])
        send(half, half, ow_send.at[2], ow_y.at[i, 2], y_last)
        send(part, part, ow_send.at[2], ow_p.at[2], partner)

    def ow_c(i):
        part = ow_pair(3, i)
        wait(part, ow_y.at[i, 2])
        send(part, part, ow_send.at[2], ow_p.at[3], partner)

    def ow_row_done(row):
        wait(ow.at[pl.ds(0, 4)], ow_p.at[row])

    def ow_sent():
        @pl.when(keeps)
        def _():
            wait(ow.at[pl.ds(0, 3)], ow_send.at[0])

        @pl.when(jnp.logical_not(keeps))
        def _():
            wait(ow.at[pl.ds(0, 4)], ow_send.at[0])

        wait(ow.at[pl.ds(0, 3)], ow_send.at[1])
        wait(ow.at[pl.ds(0, 28)], ow_send.at[2])

    def normalize(i, carry):
        rows = pl.ds(pl.multiple_of(i * 32, 32), 32)
        squares = jnp.zeros((32, 128), F32)
        for j in range(WIDTH // 128):
            v = tok[rows, j * 128 : (j + 1) * 128].astype(F32)
            squares = squares + v * v
        mean = jnp.sum(squares, axis=-1, keepdims=True) * (1.0 / WIDTH)
        scale = lax.rsqrt(mean + 1e-06)
        for j in range(WIDTH // 128):
            cols = slice(j * 128, (j + 1) * 128)
            v = tok[rows, cols].astype(F32)
            tok[rows, cols] = (v * scale * gain_ref[j : j + 1, :].astype(F32)).astype(BF16)
        return carry

    def norm(i):
        if i == 0:
            tok_copy.wait()
        lax.fori_loop(2 * i, 2 * i + 2, normalize, 0)

    my_block = cache_ref.at[:, pl.ds(pl.multiple_of(r * HEAD, HEAD), HEAD)]

    def kv_group(row):
        base = kvw_rows[row]
        if row == 0:
            kvw_own.wait()
            kvacc[...] = jnp.zeros_like(kvacc)
        kvw_row_done(row)

        def kv_product(i, carry):
            cols = pl.ds(pl.multiple_of(base * 2048 + i * 512, 512), 512)
            kvacc[...] += jnp.dot(
                tok[:, cols],
                kvw[pl.ds(base * 8 + 2 * i, 2)].reshape(512, HEAD),
                preferred_element_type=F32,
            )
            return carry

        lax.fori_loop(0, 4, kv_product, 0)

    side_head = side * KV_HEADS + lax.div(r, 2)
    first_peer = 2 * lax.rem(r, 4) + lax.div(r, 4)
    moves = first_peer != r
    all_peers = jnp.logical_not(moves)

    def cache_first():
        plain = kvacc[...] + kvb_ref[...].astype(F32)
        rotated = rotate(plain, cos_ref[...], sin_ref[...])
        my_block[...] = jnp.where(r < KV_HEADS, rotated, plain).astype(BF16)

        @pl.when(moves)
        def _():
            send(my_block, my_block, cache_send.at[0], cache_recv.at[0], (c, first_peer))

    def cache_wait():
        @pl.when(moves)
        def _():
            wait(kv_mine.at[0], cache_recv.at[0])

        column = pl.multiple_of(side_head * HEAD, HEAD)
        copy = pltpu.make_async_copy(
            cache_ref.at[:, pl.ds(column, HEAD)], kv_mine.at[c], local_sem.at[3]
        )
        copy.start()
        copy.wait()

    def cache_rest():
        for i in range(1, REP):

            @pl.when(rep_peer(i) != first_peer)
            def _():
                send(my_block, my_block, cache_send.at[1], cache_recv.at[1], (c, rep_peer(i)))

    def cache_done(sem):
        @pl.when(moves)
        def _():
            wait(kv_mine.at[pl.ds(0, 6)], sem)

        @pl.when(all_peers)
        def _():
            wait(kv_mine.at[pl.ds(0, 7)], sem)

    def q_group(row):
        base = q_rows[row]
        if row == 0:
            qw_own.wait()
            acc[...] = jnp.zeros_like(acc)
        for part in q_parts:
            part[2](row)

        def q_product(i, carry):
            cols = pl.ds(pl.multiple_of(base * 2048 + i * 512, 512), 512)
            acc[...] += jnp.dot(
                tok[:, cols],
                qw[pl.ds(base * 8 + 2 * i, 2)].reshape(512, LOCAL * HEAD),
                preferred_element_type=F32,
            )
            return carry

        lax.fori_loop(0, 4, q_product, 0)

    def q_finish():
        for h in range(LOCAL):
            v = acc[:, h * HEAD : (h + 1) * HEAD] + qb_ref[h : h + 1, :].astype(F32)
            qs[h] = rotate(v, cos_ref[...], sin_ref[...]).astype(BF16)

    def attend_row(row, heads):
        base = kv_rows[row]
        for h in heads:
            slot = h % 2
            peak = None
            for b in range(4):
                keys = kv[0, pl.ds(8 * base + 2 * b, 2)].reshape(512, HEAD)
                s = lax.dot_general(
                    qs[h], keys, (((1,), (1,)), ((), ())), preferred_element_type=F32
                )
                if row == 0:
                    key_pos = (4 * base + b) * 512 + lax.broadcasted_iota(jnp.int32, s.shape, 1)
                    query_pos = c * ROWS + lax.broadcasted_iota(jnp.int32, s.shape, 0)
                    s = jnp.where(key_pos <= query_pos, s, NEG)
                s_ref[slot, b] = s
                for t in range(4):
                    tile = s[:, t * 128 : (t + 1) * 128]
                    peak = tile if peak is None else jnp.maximum(peak, tile)
            m_new = jnp.broadcast_to(jnp.max(peak, axis=-1, keepdims=True), (ROWS, 128))
            if row == 0:
                total = jnp.zeros((ROWS, 128), F32)
                out = jnp.zeros((ROWS, HEAD), F32)
            else:
                m_old = m_ref[h]
                m_new = jnp.maximum(m_old, m_new)
                alpha = jnp.exp2((m_old - m_new) * EXP_SCALE)
                total = l_ref[h] * alpha
                out = o_ref[h] * alpha
            for b in range(4):
                values = kv[1, pl.ds(8 * base + 2 * b, 2)].reshape(512, HEAD)
                weights = []
                for t in range(4):
                    p = jnp.exp2((s_ref[slot, b, :, t * 128 : (t + 1) * 128] - m_new) * EXP_SCALE)
                    total = total + p
                    weights.append(p.astype(BF16))
                out = out + jnp.dot(
                    jnp.concatenate(weights, axis=1), values, preferred_element_type=F32
                )
            m_ref[h] = m_new
            l_ref[h] = total
            o_ref[h] = out

    def attend(row, pair):
        if pair == 0:
            kv_row_done(row)
            wait(kv_other.at[pl.ds(0, 4)], kv_recv.at[23 + row])
        heads = (2 * pair, 2 * pair + 1)
        if row == 0:
            attend_row(row, heads)
        else:
            pl.when(kv_rows[row] < zh)(functools.partial(attend_row, row, heads))

    x_next = (c, zl * 4 + lax.rem(x + 1, 4))
    x_last = (c, zl * 4 + lax.rem(x + 3, 4))

    def att_part(dx, h, half=None):
        rows = slice(None) if half is None else pl.ds(128 * half, 128)
        source = lax.rem(x + dx, 4)
        place = 2 * lax.rem(source, 2) + lax.div(source, 2)
        return att.at[rows, pl.ds(pl.multiple_of((place * LOCAL + h) * HEAD, HEAD), HEAD)]

    def att_share(h):
        part = att_part(0, h)
        total = jnp.sum(l_ref[h], axis=-1, keepdims=True)
        part[...] = (o_ref[h] / total).astype(BF16)
        send(part, part, att_send, att_x.at[h, 0], x_next)
        send(part, part, att_send, att_x.at[h, 1], x_last)

    def att_pass(h):
        wait(att_part(3, h), att_x.at[h, 0])
        half = att_part(3, h, 0)
        send(half, half, att_send, att_x.at[h, 2], x_next)
        wait(att_part(1, h), att_x.at[h, 1])
        half = att_part(1, h, 1)
        send(half, half, att_send, att_x.at[h, 2], x_last)

    def att_wait():
        for h in range(LOCAL):
            wait(att_part(2, h), att_x.at[h, 2])

    def out_block(row):
        ow_row_done(row)
        y_ = y_rows[row]
        for i in range(2):
            rows = ow[pl.ds(y_ * 8 + 4 * i, 4)].reshape(4 * LOCAL * HEAD, 256)
            part = jnp.dot(att[...], rows, preferred_element_type=F32)
            outp[row, :, i * 256 : (i + 1) * 256] = part.astype(BF16)
        for i in range(1, REP):
            peer = rep_peer(i)
            src = outp.at[row, pl.ds(pl.multiple_of(peer * 32, 32), 32)]
            send(src, part_ref.at[r, y_], a2a_send, a2a_recv.at[row], (c, peer))
        part_ref[r, y_] = outp[row, pl.ds(pl.multiple_of(r * 32, 32), 32), :]

    ops = {"cs": cache_first,
        "cr": cache_rest,
        "cw": cache_wait, "qf": q_finish, "aw": att_wait}
    for prefix, steps in (
        ("k_", kvw_steps),
        ("q_", q_parts[0][0]),
        ("p_", q_parts[1][0]),
        ("v_", kv_steps),
    ):
        ops |= {prefix + name: step for name, step in steps.items()}
    for prefix, op in (
        ("n", norm),
        ("kg", kv_group),
        ("qg", q_group),
        ("oz", oz_wait),
        ("og", oz_give),
        ("vr", kv_relay),
        ("oy", ow_y_start),
        ("ob", ow_b),
        ("ox", ow_c),
        ("as", att_share),
        ("ap", att_pass),
        ("out", out_block),
    ):
        ops |= {prefix + str(i): functools.partial(op, i) for i in range(4)}
    for i in range(2):
        ops[f"ozs{i}"] = functools.partial(oz_start, i)
    for row in range(4):
        ops |= {f"at{row}{pair}": functools.partial(attend, row, pair) for pair in range(2)}
    for name in ORDER:
        ops[name]()

    for row in range(4):
        wait(outp.at[0, pl.ds(0, 224)], a2a_recv.at[row])

    kvw_sent()
    for part in q_parts:
        part[3]()
    kv_sent()
    ow_sent()
    wait(kv_mine.at[pl.ds(0, 16)], ag_send.at[3])
    wait(kv_mine.at[pl.ds(0, 16)], ag_send.at[4])
    cache_done(cache_send.at[1])
    cache_done(cache_recv.at[1])

    @pl.when(moves)
    def _():
        wait(kv_mine.at[0], cache_send.at[0])

    wait(att.at[:, pl.ds(0, 12 * HEAD)], att_send)
    wait(kv_mine.at[pl.ds(0, 14)], a2a_send)


def hand_over(part_in, cache_in, out_ref, cache_ref):
    for x in range(4):
        for zh in range(4):
            place = (x - zh) % 4
            for y in range(4):
                column = ctx_of(zh, y, place // 2) * 256 + place % 2 * 128
                cols = slice(zh * 128, (zh + 1) * 128)
                total = part_in[x, y, :, cols].astype(F32) + part_in[4 + x, y, :, cols].astype(F32)
                out_ref[:, column : column + 128] = total.astype(BF16)
    cache_ref[...] = cache_in[...]


def per_device(tokens, norm_gain, q_weight, q_bias, key_value_weight, kv_bias, out_weight):
    positions = lax.axis_index("ctx") * ROWS + jnp.arange(ROWS, dtype=jnp.int32)
    half = HEAD // 2
    exponent = jnp.arange(half, dtype=F32) * (2.0 / HEAD)
    inverse = ROPE_BASE ** (-exponent)
    angles = positions.astype(F32)[:, None] * inverse[None, :]
    cosine, sine = jnp.cos(angles), jnp.sin(angles)
    cos = jnp.concatenate([cosine, cosine], axis=-1)
    sin = jnp.concatenate([-sine, sine], axis=-1)
    any_spec = pl.BlockSpec(memory_space=pl.ANY)
    vmem_spec = pl.BlockSpec(memory_space=pltpu.VMEM)
    dma = pltpu.SemaphoreType.DMA
    parts, cache = pl.pallas_call(
        kernel,
        out_shape=(
            jax.ShapeDtypeStruct((REP, 4, ROWS // REP, 512), BF16),
            jax.ShapeDtypeStruct((ROWS, 2 * KV_HEADS * HEAD), BF16),
        ),
        in_specs=[any_spec] * 4 + [vmem_spec] * 5,
        out_specs=(vmem_spec, vmem_spec),
        scratch_shapes=[
            pltpu.VMEM((ROWS, WIDTH), BF16),
            pltpu.VMEM((CTX, 256, LOCAL * HEAD), BF16),
            pltpu.VMEM((CTX, 256, HEAD), BF16),
            pltpu.VMEM((2, CTX, ROWS, HEAD), BF16),
            pltpu.VMEM((CTX, LOCAL * HEAD, 256), BF16),
            pltpu.VMEM((4, LOCAL * HEAD, 256), BF16),
            pltpu.VMEM((ROWS, 4 * LOCAL * HEAD), BF16),
            pltpu.VMEM((4, ROWS, 512), BF16),
            pltpu.VMEM((LOCAL, ROWS, HEAD), BF16),
            pltpu.VMEM((ROWS, LOCAL * HEAD), F32),
            pltpu.VMEM((ROWS, HEAD), F32),
            pltpu.VMEM((2, 4, ROWS, 512), F32),
            pltpu.VMEM((LOCAL, ROWS, HEAD), F32),
            pltpu.VMEM((LOCAL, ROWS, HEAD), F32),
            pltpu.VMEM((LOCAL, ROWS, HEAD), F32),
            dma((4,)),
            dma((6,)),
            dma((19,)),
            dma((2, 19)),
            dma((27,)),
            dma((2,)),
            dma((2,)),
            dma((3,)),
            dma((3,)),
            dma((4,)),
            dma((4, 3)),
            dma((4,)),
            dma,
            dma((4, 3)),
            dma,
            dma((4,)),
        ],
        compiler_params=pltpu.CompilerParams(
            collective_id=0, has_side_effects=True, vmem_limit_bytes=60 << 20
        ),
    )(
        tokens,
        q_weight,
        key_value_weight,
        out_weight,
        norm_gain.reshape(WIDTH // HEAD, HEAD),
        cos,
        sin,
        q_bias.reshape(LOCAL, HEAD),
        kv_bias.reshape(1, HEAD),
    )
    return pl.pallas_call(
        hand_over,
        out_shape=(
            jax.ShapeDtypeStruct((ROWS // REP, WIDTH), BF16),
            jax.ShapeDtypeStruct(cache.shape, BF16),
        ),
        in_specs=[vmem_spec, vmem_spec],
        out_specs=(vmem_spec, vmem_spec),
    )(parts, cache)


def solution(mesh):
    in_specs = (
        P("ctx", None),
        P(),
        P("ctx", "rep"),
        P("rep"),
        P("ctx", "rep"),
        P("rep"),
        P("rep", "ctx"),
    )
    out_specs = (P(("ctx", "rep"), None), P("ctx", None))
    return jax.shard_map(
        per_device, mesh=mesh, in_specs=in_specs, out_specs=out_specs, check_vma=False
    )
```

```python
import functools

import jax
import jax.numpy as jnp
from jax import lax
from jax.experimental import pallas as pl
from jax.experimental.pallas import tpu as pltpu
from jax.sharding import PartitionSpec as P

MESH = pl.DeviceIdType.MESH
F32 = jnp.float32
BF16 = jnp.bfloat16

HEAD = 128
Q_HEADS = 32
KV_HEADS = 4
ROWS = 256
WIDTH = 8192
CTX = 32
REP = 8
LOCAL = Q_HEADS // REP
ROPE_BASE = 1000000.0
EXP_SCALE = HEAD ** (-0.5) * 1.4426950408889634
NEG = -1e30

ORDER = (
    "k_t", "k_s", "n0", "p_s", "q_t", "k_r0", "p_t", "n1", "k_x0", "k_b",
    "k_a", "q_r0", "q_s", "k_r2", "k_c", "k_r1", "n2", "n3", "p_r0", "kg0",
    "og0", "k_x2", "k_r3", "p_b", "ozs0", "k_x1", "k_x3", "q_b", "q_x0", "q_a",
    "kg2", "kg1", "p_x0", "kg3", "cs", "q_r2", "cw", "v_t", "v_s", "p_a",
    "qg0", "p_r2", "v_r0", "ozs1", "q_r1", "v_a", "p_r1", "v_x0", "v_b", "q_x2",
    "p_c", "q_x1", "p_x2", "q_c", "v_r1", "v_r2", "v_c", "p_x1", "oz2", "vr0",
    "oz1", "og1", "og2", "p_r3", "q_r3", "v_x2", "v_r3", "oy0", "p_x3", "q_x3",
    "qg2", "oz3", "v_x3", "vr2", "v_x1", "og3", "qg1", "oy1", "qg3", "qf",
    "cr", "at00", "vr3", "at20", "vr1", "oy2", "at01", "at30", "oy3", "ob1",
    "at10", "as1", "as0", "ob0", "at31", "at11", "at21", "as2", "as3", "ap1",
    "ob2", "ap0", "ap2", "ob3", "ap3", "cf", "aw", "out0", "out1", "out2",
    "ox1", "ox0", "ox2", "ox3", "out3",
)


def ctx_of(zh, y, k):
    return zh * 8 + y * 2 + k


def send(src, dst, send_sem, recv_sem, device):
    pltpu.make_async_remote_copy(
        src_ref=src,
        dst_ref=dst,
        send_sem=send_sem,
        recv_sem=recv_sem,
        device_id=device,
        device_id_type=MESH,
    ).start()


def wait(ref, sem):
    pltpu.make_async_copy(ref, ref, sem).wait()


def rotate(v, cos, sin):
    return v * cos + pltpu.roll(v, HEAD // 2, 1) * sin


def gather_steps(buf, own, halves, z_first, where, send_sem, recv_sem, beside=None, beside_send=None):
    zh, y, k, r = where
    a, b = (zh, y) if z_first else (y, zh)

    def slot(a_, b_, k_=k):
        return ctx_of(a_, b_, k_) if z_first else ctx_of(b_, a_, k_)

    def device(da, db):
        return (slot(lax.rem(a + da, 4), lax.rem(b + db, 4)), r)

    partner = (slot(a, b, 1 - k), r)
    rows = (a, lax.rem(a + 3, 4), lax.rem(a + 1, 4), lax.rem(a + 2, 4))
    before, after, across = lax.rem(b + 3, 4), lax.rem(b + 1, 4), lax.rem(b + 2, 4)

    def full(s, sem, dev, src=None):
        send(buf.at[s] if src is None else src, buf.at[s], send_sem, recv_sem.at[sem], dev)

    def half(s, which, sem, dev):
        send(halves(s, which), halves(s, which), send_sem, recv_sem.at[sem], dev)

    def arrived(s, sem):
        wait(buf.at[s], recv_sem.at[sem])

    def share(s, row, src=None):
        full(s, 15 + row, partner, src)
        if beside is not None:
            send(buf.at[s] if src is None else src, buf.at[s], beside_send, recv_sem.at[19 + row], beside)

    def spread(row, src=None):
        s = slot(rows[row], b)
        full(s, 3 + 3 * row, device(0, 1), src)
        full(s, 4 + 3 * row, device(0, 3), src)
        share(s, row, src)

    def start_first():
        s = slot(a, b)
        full(s, 0, device(1, 0), own)
        full(s, 1, device(3, 0), own)

    def start_second():
        spread(0, own)

    def first_before():
        s = slot(rows[1], b)
        arrived(s, 0)
        half(s, 0, 2, device(1, 0))
        spread(1)

    def first_after():
        s = slot(rows[2], b)
        arrived(s, 1)
        half(s, 1, 2, device(3, 0))
        spread(2)

    def first_across():
        arrived(slot(rows[3], b), 2)
        spread(3)

    def second(row):
        def step():
            s = slot(rows[row], before)
            arrived(s, 3 + 3 * row)
            half(s, 0, 5 + 3 * row, device(0, 1))
            share(s, row)
            s = slot(rows[row], after)
            arrived(s, 4 + 3 * row)
            half(s, 1, 5 + 3 * row, device(0, 3))
            share(s, row)

        return step

    def second_across(row):
        def step():
            s = slot(rows[row], across)
            arrived(s, 5 + 3 * row)
            share(s, row)

        return step

    steps = {
        "s": start_first,
        "t": start_second,
        "a": first_before,
        "b": first_after,
        "c": first_across,
        "r0": second(0),
        "r1": second(1),
        "r2": second(2),
        "r3": second(3),
        "x0": second_across(0),
        "x1": second_across(1),
        "x2": second_across(2),
        "x3": second_across(3),
    }

    def row_done(row):
        wait(buf.at[pl.ds(0, 4)], recv_sem.at[15 + row])

    def sent():
        wait(buf.at[pl.ds(0, 31)], send_sem)

    return steps, rows, row_done, sent


def kernel(
    tok_hbm,
    qw_hbm,
    kvw_hbm,
    ow_hbm,
    gain_hbm,
    cos_hbm,
    sin_hbm,
    qb_hbm,
    kvb_hbm,
    part_ref,
    cache_out,
    cache_ref,
    gain_ref,
    cos_ref,
    sin_ref,
    qb_ref,
    kvb_ref,
    tok,
    qw,
    kvw,
    kv,
    ow,
    oz,
    att,
    outp,
    qs,
    acc,
    kvacc,
    s_ref,
    m_ref,
    l_ref,
    o_ref,
    local_sem,
    ag_send,
    kvw_recv,
    qw_recv,
    kv_recv,
    cache_send,
    cache_recv,
    ow_send,
    oz_recv,
    ow_z,
    ow_y,
    ow_p,
    att_send,
    att_x,
    a2a_send,
    a2a_recv,
):
    c = lax.axis_index("ctx")
    r = lax.axis_index("rep")
    k = lax.rem(c, 2)
    y = lax.rem(lax.div(c, 2), 4)
    zh = lax.div(c, 8)
    x = lax.rem(r, 4)
    zl = lax.div(r, 4)
    where = (zh, y, k, r)
    c_pair = c - k

    def rep_peer(i):
        return lax.rem(r + i, REP)

    tok_copy = pltpu.make_async_copy(tok_hbm, tok, local_sem.at[0])
    tok_copy.start()
    kvw_own = pltpu.make_async_copy(kvw_hbm, kvw.at[c], local_sem.at[1])
    kvw_own.start()
    qw_own = pltpu.make_async_copy(qw_hbm, qw.at[c], local_sem.at[2])
    qw_own.start()

    small = []
    for i, (src, dst) in enumerate(
        (
            (gain_hbm, gain_ref),
            (cos_hbm, cos_ref),
            (sin_hbm, sin_ref),
            (qb_hbm, qb_ref),
            (kvb_hbm, kvb_ref),
        )
    ):
        small.append(pltpu.make_async_copy(src, dst, local_sem.at[4 + i]))
        small[-1].start()

    barrier = pltpu.get_barrier_semaphore()
    greet = [(c_pair + k, rep_peer(i)) for i in range(1, REP)]
    greet += [(c_pair + 1 - k, zl * 4 + lax.rem(x + i, 4)) for i in range(4)]
    greet += [(ctx_of(zh, lax.rem(y + d, 4), k), r) for d in (1, 3)]
    greet += [(ctx_of(lax.rem(zh + d, 4), y, k), r) for d in (1, 3)]
    for dev in greet:
        pl.semaphore_signal(barrier, inc=1, device_id=dev, device_id_type=MESH)
    pl.semaphore_wait(barrier, len(greet))

    kvw_steps, kvw_rows, kvw_row_done, kvw_sent = gather_steps(
        kvw, kvw_hbm, lambda s, i: kvw.at[s, pl.ds(128 * i, 128)], True, where, ag_send.at[0], kvw_recv
    )
    q_parts = []
    for i in range(2):
        view = qw.at[:, pl.ds(128 * i, 128)]
        q_parts.append(
            gather_steps(
                view,
                qw_hbm.at[pl.ds(128 * i, 128)],
                lambda s, j, i=i: qw.at[s, pl.ds(128 * i + 64 * j, 64)],
                True,
                where,
                ag_send.at[1 + 4 * i],
                qw_recv.at[i],
            )
        )
    q_rows = q_parts[0][1]
    side = lax.rem(r, 2)
    beside = (c, r + 1 - 2 * side)
    kv_mine, kv_other = kv.at[side], kv.at[1 - side]
    kv_steps, kv_rows, kv_row_done, kv_sent = gather_steps(
        kv_mine,
        None,
        lambda s, i: kv_mine.at[s, pl.ds(128 * i, 128)],
        True,
        where,
        ag_send.at[2],
        kv_recv,
        beside,
        ag_send.at[4],
    )

    def kv_relay(row):
        wait(kv_other.at[pl.ds(0, 4)], kv_recv.at[19 + row])
        for i in range(4):
            s = ctx_of(kv_rows[row], i, k)
            send(
                kv_other.at[s],
                kv_other.at[s],
                ag_send.at[3],
                kv_recv.at[23 + row],
                (ctx_of(zh, y, 1 - k), r),
            )

    z_next = (ctx_of(lax.rem(zh + 1, 4), y, k), r)
    z_last = (ctx_of(lax.rem(zh + 3, 4), y, k), r)
    y_next = (ctx_of(zh, lax.rem(y + 1, 4), k), r)
    y_last = (ctx_of(zh, lax.rem(y + 3, 4), k), r)
    partner = (ctx_of(zh, y, 1 - k), r)
    y_rows = (y, lax.rem(y + 3, 4), lax.rem(y + 1, 4), lax.rem(y + 2, 4))
    z_rows = (zh, lax.rem(zh + 3, 4), lax.rem(zh + 1, 4), lax.rem(zh + 2, 4))
    keeps = lax.rem(x, 2) == k

    def ow_place(y_, z_, first, count):
        cols = pl.ds(pl.multiple_of(128 * lax.rem(z_, 2), 128), 128)
        return ow.at[pl.ds(y_ * 8 + lax.div(z_, 2) * 4 + first, count), :, cols]

    def ow_pair(y_row, row):
        return ow_place(y_rows[y_row], z_rows[row], 2 * k, 2)

    def ow_half(y_row, row, i):
        return ow_place(y_rows[y_row], z_rows[row], 2 * k + i, 1)

    def oz_half(s, i):
        return oz.at[s, pl.ds(256 * i, 256)]

    def oz_start(i):
        rows = pl.ds(256 * i, 256)
        send(ow_hbm.at[rows], oz.at[zh, rows], ow_send.at[1], oz_recv.at[0], z_next)
        send(ow_hbm.at[rows], oz.at[zh, rows], ow_send.at[1], oz_recv.at[1], z_last)

    def oz_wait(row):
        s = z_rows[row]
        wait(oz.at[s], oz_recv.at[row - 1])
        if row == 1:
            send(oz_half(s, 0), oz_half(s, 0), ow_send.at[1], oz_recv.at[2], z_next)
        if row == 2:
            send(oz_half(s, 1), oz_half(s, 1), ow_send.at[1], oz_recv.at[2], z_last)

    def oz_give(row):
        z_ = z_rows[row]
        src = ow_hbm if row == 0 else oz.at[z_]
        spot = y * 8 + lax.div(z_, 2) * 4 + 2 * lax.rem(x, 2) + lax.div(x, 2)
        dst = ow.at[spot, :, pl.ds(pl.multiple_of(128 * lax.rem(z_, 2), 128), 128)]
        for j in range(2):
            worker = lax.rem(2 * k + j + z_, 4)
            part = src.at[:, pl.ds(128 * j, 128)]
            here = (worker == x) & keeps

            @pl.when(here)
            def _(part=part):
                pltpu.make_async_copy(part, dst, ow_z.at[row]).start()

            @pl.when(jnp.logical_not(here))
            def _(part=part, worker=worker):
                device = (ctx_of(zh, y, lax.rem(x, 2)), zl * 4 + worker)
                send(part, dst, ow_send.at[0], ow_z.at[row], device)

    def ow_y_start(i):
        part = ow_pair(0, i)
        wait(part, ow_z.at[i])
        send(part, part, ow_send.at[2], ow_y.at[i, 0], y_next)
        send(part, part, ow_send.at[2], ow_y.at[i, 1], y_last)
        send(part, part, ow_send.at[2], ow_p.at[0], partner)

    def ow_b(i):
        part, half = ow_pair(1, i), ow_half(1, i, 0)
        wait(part, ow_y.at[i, 0])
        send(half, half, ow_send.at[2], ow_y.at[i, 2], y_next)
        send(part, part, ow_send.at[2], ow_p.at[1], partner)
        part, half = ow_pair(2, i), ow_half(2, i, 1)
        wait(part, ow_y.at[i, 1])
        send(half, half, ow_send.at[2], ow_y.at[i, 2], y_last)
        send(part, part, ow_send.at[2], ow_p.at[2], partner)

    def ow_c(i):
        part = ow_pair(3, i)
        wait(part, ow_y.at[i, 2])
        send(part, part, ow_send.at[2], ow_p.at[3], partner)

    def ow_row_done(row):
        wait(ow.at[pl.ds(0, 4)], ow_p.at[row])

    def ow_sent():
        @pl.when(keeps)
        def _():
            wait(ow.at[pl.ds(0, 3)], ow_send.at[0])

        @pl.when(jnp.logical_not(keeps))
        def _():
            wait(ow.at[pl.ds(0, 4)], ow_send.at[0])

        wait(ow.at[pl.ds(0, 3)], ow_send.at[1])
        wait(ow.at[pl.ds(0, 28)], ow_send.at[2])

    def normalize(i, carry):
        rows = pl.ds(pl.multiple_of(i * 32, 32), 32)
        squares = jnp.zeros((32, 128), F32)
        for j in range(WIDTH // 128):
            v = tok[rows, j * 128 : (j + 1) * 128].astype(F32)
            squares = squares + v * v
        mean = jnp.sum(squares, axis=-1, keepdims=True) * (1.0 / WIDTH)
        scale = lax.rsqrt(mean + 1e-06)
        for j in range(WIDTH // 128):
            cols = slice(j * 128, (j + 1) * 128)
            v = tok[rows, cols].astype(F32)
            tok[rows, cols] = (v * scale * gain_ref[j : j + 1, :].astype(F32)).astype(BF16)
        return carry

    def norm(i):
        if i == 0:
            tok_copy.wait()
            for copy in small:
                copy.wait()
        lax.fori_loop(2 * i, 2 * i + 2, normalize, 0)

    my_block = cache_ref.at[:, pl.ds(pl.multiple_of(r * HEAD, HEAD), HEAD)]

    def kv_group(row):
        base = kvw_rows[row]
        if row == 0:
            kvw_own.wait()
            kvacc[...] = jnp.zeros_like(kvacc)
        kvw_row_done(row)

        def kv_product(i, carry):
            cols = pl.ds(pl.multiple_of(base * 2048 + i * 512, 512), 512)
            kvacc[...] += jnp.dot(
                tok[:, cols],
                kvw[pl.ds(base * 8 + 2 * i, 2)].reshape(512, HEAD),
                preferred_element_type=F32,
            )
            return carry

        lax.fori_loop(0, 4, kv_product, 0)

    side_head = side * KV_HEADS + lax.div(r, 2)
    first_peer = 2 * lax.rem(r, 4) + lax.div(r, 4)
    moves = first_peer != r
    all_peers = jnp.logical_not(moves)

    def cache_first():
        plain = kvacc[...] + kvb_ref[...].astype(F32)
        rotated = rotate(plain, cos_ref[...], sin_ref[...])
        my_block[...] = jnp.where(r < KV_HEADS, rotated, plain).astype(BF16)

        @pl.when(moves)
        def _():
            send(my_block, my_block, cache_send.at[0], cache_recv.at[0], (c, first_peer))

    def cache_wait():
        @pl.when(moves)
        def _():
            wait(kv_mine.at[0], cache_recv.at[0])

        column = pl.multiple_of(side_head * HEAD, HEAD)
        copy = pltpu.make_async_copy(
            cache_ref.at[:, pl.ds(column, HEAD)], kv_mine.at[c], local_sem.at[3]
        )
        copy.start()
        copy.wait()

    def cache_rest():
        for i in range(1, REP):

            @pl.when(rep_peer(i) != first_peer)
            def _():
                send(my_block, my_block, cache_send.at[1], cache_recv.at[1], (c, rep_peer(i)))

    def cache_done(sem):
        @pl.when(moves)
        def _():
            wait(kv_mine.at[pl.ds(0, 6)], sem)

        @pl.when(all_peers)
        def _():
            wait(kv_mine.at[pl.ds(0, 7)], sem)

    def q_group(row):
        base = q_rows[row]
        if row == 0:
            qw_own.wait()
            acc[...] = jnp.zeros_like(acc)
        for part in q_parts:
            part[2](row)

        def q_product(i, carry):
            cols = pl.ds(pl.multiple_of(base * 2048 + i * 512, 512), 512)
            acc[...] += jnp.dot(
                tok[:, cols],
                qw[pl.ds(base * 8 + 2 * i, 2)].reshape(512, LOCAL * HEAD),
                preferred_element_type=F32,
            )
            return carry

        lax.fori_loop(0, 4, q_product, 0)

    def q_finish():
        for h in range(LOCAL):
            v = acc[:, h * HEAD : (h + 1) * HEAD] + qb_ref[h : h + 1, :].astype(F32)
            qs[h] = rotate(v, cos_ref[...], sin_ref[...]).astype(BF16)

    def attend_row(row, heads):
        base = kv_rows[row]
        for h in heads:
            slot = h % 2
            peak = None
            for b in range(4):
                keys = kv[0, pl.ds(8 * base + 2 * b, 2)].reshape(512, HEAD)
                s = lax.dot_general(
                    qs[h], keys, (((1,), (1,)), ((), ())), preferred_element_type=F32
                )
                if row == 0:
                    key_pos = (4 * base + b) * 512 + lax.broadcasted_iota(jnp.int32, s.shape, 1)
                    query_pos = c * ROWS + lax.broadcasted_iota(jnp.int32, s.shape, 0)
                    s = jnp.where(key_pos <= query_pos, s, NEG)
                s_ref[slot, b] = s
                for t in range(4):
                    tile = s[:, t * 128 : (t + 1) * 128]
                    peak = tile if peak is None else jnp.maximum(peak, tile)
            m_new = jnp.broadcast_to(jnp.max(peak, axis=-1, keepdims=True), (ROWS, 128))
            if row == 0:
                total = jnp.zeros((ROWS, 128), F32)
                out = jnp.zeros((ROWS, HEAD), F32)
            else:
                m_old = m_ref[h]
                m_new = jnp.maximum(m_old, m_new)
                alpha = jnp.exp2((m_old - m_new) * EXP_SCALE)
                total = l_ref[h] * alpha
                out = o_ref[h] * alpha
            for b in range(4):
                values = kv[1, pl.ds(8 * base + 2 * b, 2)].reshape(512, HEAD)
                weights = []
                for t in range(4):
                    p = jnp.exp2((s_ref[slot, b, :, t * 128 : (t + 1) * 128] - m_new) * EXP_SCALE)
                    total = total + p
                    weights.append(p.astype(BF16))
                out = out + jnp.dot(
                    jnp.concatenate(weights, axis=1), values, preferred_element_type=F32
                )
            m_ref[h] = m_new
            l_ref[h] = total
            o_ref[h] = out

    def attend(row, pair):
        if pair == 0:
            kv_row_done(row)
            wait(kv_other.at[pl.ds(0, 4)], kv_recv.at[23 + row])
        heads = (2 * pair, 2 * pair + 1)
        if row == 0:
            attend_row(row, heads)
        else:
            pl.when(kv_rows[row] < zh)(functools.partial(attend_row, row, heads))

    x_next = (c, zl * 4 + lax.rem(x + 1, 4))
    x_last = (c, zl * 4 + lax.rem(x + 3, 4))

    def att_part(dx, h, half=None):
        rows = slice(None) if half is None else pl.ds(128 * half, 128)
        source = lax.rem(x + dx, 4)
        place = 2 * lax.rem(source, 2) + lax.div(source, 2)
        return att.at[rows, pl.ds(pl.multiple_of((place * LOCAL + h) * HEAD, HEAD), HEAD)]

    def att_share(h):
        part = att_part(0, h)
        total = jnp.sum(l_ref[h], axis=-1, keepdims=True)
        part[...] = (o_ref[h] / total).astype(BF16)
        send(part, part, att_send, att_x.at[h, 0], x_next)
        send(part, part, att_send, att_x.at[h, 1], x_last)

    def att_pass(h):
        wait(att_part(3, h), att_x.at[h, 0])
        half = att_part(3, h, 0)
        send(half, half, att_send, att_x.at[h, 2], x_next)
        wait(att_part(1, h), att_x.at[h, 1])
        half = att_part(1, h, 1)
        send(half, half, att_send, att_x.at[h, 2], x_last)

    def att_wait():
        for h in range(LOCAL):
            wait(att_part(2, h), att_x.at[h, 2])

    def own_part(row):
        src = outp.at[row, pl.ds(pl.multiple_of(r * 32, 32), 32)]
        return pltpu.make_async_copy(src, part_ref.at[r, y_rows[row]], local_sem.at[9 + row])

    cache_copy = pltpu.make_async_copy(cache_ref, cache_out, local_sem.at[13])

    def cache_finish():
        cache_done(cache_recv.at[1])
        cache_copy.start()

    def out_block(row):
        ow_row_done(row)
        y_ = y_rows[row]
        for i in range(2):
            rows = ow[pl.ds(y_ * 8 + 4 * i, 4)].reshape(4 * LOCAL * HEAD, 256)
            part = jnp.dot(att[...], rows, preferred_element_type=F32)
            outp[row, :, i * 256 : (i + 1) * 256] = part.astype(BF16)
        for i in range(1, REP):
            peer = rep_peer(i)
            src = outp.at[row, pl.ds(pl.multiple_of(peer * 32, 32), 32)]
            send(src, part_ref.at[r, y_], a2a_send, a2a_recv.at[row], (c, peer))
        own_part(row).start()

    ops = {"cs": cache_first,
        "cr": cache_rest,
        "cf": cache_finish,
        "cw": cache_wait, "qf": q_finish, "aw": att_wait}
    for prefix, steps in (
        ("k_", kvw_steps),
        ("q_", q_parts[0][0]),
        ("p_", q_parts[1][0]),
        ("v_", kv_steps),
    ):
        ops |= {prefix + name: step for name, step in steps.items()}
    for prefix, op in (
        ("n", norm),
        ("kg", kv_group),
        ("qg", q_group),
        ("oz", oz_wait),
        ("og", oz_give),
        ("vr", kv_relay),
        ("oy", ow_y_start),
        ("ob", ow_b),
        ("ox", ow_c),
        ("as", att_share),
        ("ap", att_pass),
        ("out", out_block),
    ):
        ops |= {prefix + str(i): functools.partial(op, i) for i in range(4)}
    for i in range(2):
        ops[f"ozs{i}"] = functools.partial(oz_start, i)
    for row in range(4):
        ops |= {f"at{row}{pair}": functools.partial(attend, row, pair) for pair in range(2)}
    for name in ORDER:
        ops[name]()

    for row in range(4):
        wait(outp.at[0, pl.ds(0, 224)], a2a_recv.at[row])

    kvw_sent()
    for part in q_parts:
        part[3]()
    kv_sent()
    ow_sent()
    wait(kv_mine.at[pl.ds(0, 16)], ag_send.at[3])
    wait(kv_mine.at[pl.ds(0, 16)], ag_send.at[4])
    cache_done(cache_send.at[1])
    cache_copy.wait()
    for row in range(4):
        own_part(row).wait()

    @pl.when(moves)
    def _():
        wait(kv_mine.at[0], cache_send.at[0])

    wait(att.at[:, pl.ds(0, 12 * HEAD)], att_send)
    wait(kv_mine.at[pl.ds(0, 14)], a2a_send)


def hand_over(part_in, cache_in, out_ref, cache_ref):
    for x in range(4):
        for zh in range(4):
            place = (x - zh) % 4
            for y in range(4):
                column = ctx_of(zh, y, place // 2) * 256 + place % 2 * 128
                cols = slice(zh * 128, (zh + 1) * 128)
                total = part_in[x, y, :, cols].astype(F32) + part_in[4 + x, y, :, cols].astype(F32)
                out_ref[:, column : column + 128] = total.astype(BF16)
    cache_ref[...] = cache_in[...]


def per_device(tokens, norm_gain, q_weight, q_bias, key_value_weight, kv_bias, out_weight):
    positions = lax.axis_index("ctx") * ROWS + jnp.arange(ROWS, dtype=jnp.int32)
    lane = jnp.arange(HEAD, dtype=jnp.int32)
    exponent = lax.rem(lane, HEAD // 2).astype(F32) * (2.0 / HEAD)
    inverse = ROPE_BASE ** (-exponent)
    angles = positions.astype(F32)[:, None] * inverse[None, :]
    cos = jnp.cos(angles)
    sin = jnp.where(lane[None, :] < HEAD // 2, -jnp.sin(angles), jnp.sin(angles))
    any_spec = pl.BlockSpec(memory_space=pl.ANY)
    vmem_spec = pl.BlockSpec(memory_space=pltpu.VMEM)
    dma = pltpu.SemaphoreType.DMA
    parts, cache = pl.pallas_call(
        kernel,
        out_shape=(
            jax.ShapeDtypeStruct((REP, 4, ROWS // REP, 512), BF16),
            jax.ShapeDtypeStruct((ROWS, 2 * KV_HEADS * HEAD), BF16),
        ),
        in_specs=[any_spec] * 9,
        out_specs=(any_spec, any_spec),
        scratch_shapes=[
            pltpu.VMEM((ROWS, 2 * KV_HEADS * HEAD), BF16),
            pltpu.VMEM((WIDTH // HEAD, HEAD), BF16),
            pltpu.VMEM((ROWS, HEAD), F32),
            pltpu.VMEM((ROWS, HEAD), F32),
            pltpu.VMEM((LOCAL, HEAD), BF16),
            pltpu.VMEM((1, HEAD), BF16),
            pltpu.VMEM((ROWS, WIDTH), BF16),
            pltpu.VMEM((CTX, 256, LOCAL * HEAD), BF16),
            pltpu.VMEM((CTX, 256, HEAD), BF16),
            pltpu.VMEM((2, CTX, ROWS, HEAD), BF16),
            pltpu.VMEM((CTX, LOCAL * HEAD, 256), BF16),
            pltpu.VMEM((4, LOCAL * HEAD, 256), BF16),
            pltpu.VMEM((ROWS, 4 * LOCAL * HEAD), BF16),
            pltpu.VMEM((4, ROWS, 512), BF16),
            pltpu.VMEM((LOCAL, ROWS, HEAD), BF16),
            pltpu.VMEM((ROWS, LOCAL * HEAD), F32),
            pltpu.VMEM((ROWS, HEAD), F32),
            pltpu.VMEM((2, 4, ROWS, 512), F32),
            pltpu.VMEM((LOCAL, ROWS, HEAD), F32),
            pltpu.VMEM((LOCAL, ROWS, HEAD), F32),
            pltpu.VMEM((LOCAL, ROWS, HEAD), F32),
            dma((14,)),
            dma((6,)),
            dma((19,)),
            dma((2, 19)),
            dma((27,)),
            dma((2,)),
            dma((2,)),
            dma((3,)),
            dma((3,)),
            dma((4,)),
            dma((4, 3)),
            dma((4,)),
            dma,
            dma((4, 3)),
            dma,
            dma((4,)),
        ],
        compiler_params=pltpu.CompilerParams(
            collective_id=0, has_side_effects=True, vmem_limit_bytes=60 << 20
        ),
    )(
        tokens,
        q_weight,
        key_value_weight,
        out_weight,
        norm_gain.reshape(WIDTH // HEAD, HEAD),
        cos,
        sin,
        q_bias.reshape(LOCAL, HEAD),
        kv_bias.reshape(1, HEAD),
    )
    return pl.pallas_call(
        hand_over,
        out_shape=(
            jax.ShapeDtypeStruct((ROWS // REP, WIDTH), BF16),
            jax.ShapeDtypeStruct(cache.shape, BF16),
        ),
        in_specs=[vmem_spec, vmem_spec],
        out_specs=(vmem_spec, vmem_spec),
    )(parts, cache)


def solution(mesh):
    in_specs = (
        P("ctx", None),
        P(),
        P("ctx", "rep"),
        P("rep"),
        P("ctx", "rep"),
        P("rep"),
        P("rep", "ctx"),
    )
    out_specs = (P(("ctx", "rep"), None), P("ctx", None))
    return jax.shard_map(
        per_device, mesh=mesh, in_specs=in_specs, out_specs=out_specs, check_vma=False
    )
```

```python
import functools

import jax
import jax.numpy as jnp
from jax import lax
from jax.experimental import pallas as pl
from jax.experimental.pallas import tpu as pltpu
from jax.sharding import PartitionSpec as P

MESH = pl.DeviceIdType.MESH
F32 = jnp.float32
BF16 = jnp.bfloat16

HEAD = 128
Q_HEADS = 32
KV_HEADS = 4
ROWS = 256
WIDTH = 8192
CTX = 32
REP = 8
LOCAL = Q_HEADS // REP
ROPE_BASE = 1000000.0
EXP_SCALE = HEAD ** (-0.5) * 1.4426950408889634
NEG = -1e30

ORDER = (
    "k_t", "k_s", "n0", "p_s", "q_t", "k_r0", "k_b", "k_a", "p_t", "n1",
    "k_x0", "q_r0", "q_s", "k_r2", "k_c", "k_r1", "n2", "n3", "p_r0", "kg0",
    "og0", "k_x2", "k_r3", "p_b", "ozs0", "k_x1", "k_x3", "q_b", "q_x0", "q_a",
    "kg2", "kg1", "p_x0", "kg3", "cs", "q_r2", "cw", "v_t", "v_s", "p_a",
    "qg0", "p_r2", "v_r0", "ozs1", "q_r1", "v_a", "p_r1", "v_x0", "v_b", "q_x2",
    "p_c", "q_x1", "p_x2", "q_c", "v_r1", "v_r2", "v_c", "p_x1", "oz2", "vr0",
    "oz1", "og1", "og2", "p_r3", "q_r3", "v_x2", "v_r3", "oy0", "p_x3", "q_x3",
    "qg2", "oz3", "v_x3", "vr2", "v_x1", "og3", "qg1", "oy1", "qg3", "qf",
    "cr", "at00", "vr3", "at20", "vr1", "oy2", "at01", "at30", "oy3", "ob1",
    "at10", "as1", "as0", "ob0", "at31", "at11", "at21", "as2", "as3", "ap1",
    "ob2", "ap0", "ap2", "ob3", "ap3", "cf", "aw", "out0", "out1", "out2",
    "ox1", "ox0", "ox2", "ox3", "out3",
)


def ctx_of(zh, y, k):
    return zh * 8 + y * 2 + k


def send(src, dst, send_sem, recv_sem, device):
    pltpu.make_async_remote_copy(
        src_ref=src,
        dst_ref=dst,
        send_sem=send_sem,
        recv_sem=recv_sem,
        device_id=device,
        device_id_type=MESH,
    ).start()


def wait(ref, sem):
    pltpu.make_async_copy(ref, ref, sem).wait()


def rotate(v, cos, sin):
    return v * cos + pltpu.roll(v, HEAD // 2, 1) * sin


def gather_steps(buf, own, halves, z_first, where, send_sem, recv_sem, beside=None, beside_send=None):
    zh, y, k, r = where
    a, b = (zh, y) if z_first else (y, zh)

    def slot(a_, b_, k_=k):
        return ctx_of(a_, b_, k_) if z_first else ctx_of(b_, a_, k_)

    def device(da, db):
        return (slot(lax.rem(a + da, 4), lax.rem(b + db, 4)), r)

    partner = (slot(a, b, 1 - k), r)
    rows = (a, lax.rem(a + 3, 4), lax.rem(a + 1, 4), lax.rem(a + 2, 4))
    before, after, across = lax.rem(b + 3, 4), lax.rem(b + 1, 4), lax.rem(b + 2, 4)

    def full(s, sem, dev, src=None):
        send(buf.at[s] if src is None else src, buf.at[s], send_sem, recv_sem.at[sem], dev)

    def half(s, which, sem, dev):
        send(halves(s, which), halves(s, which), send_sem, recv_sem.at[sem], dev)

    def arrived(s, sem):
        wait(buf.at[s], recv_sem.at[sem])

    def share(s, row, src=None):
        full(s, 15 + row, partner, src)
        if beside is not None:
            send(buf.at[s] if src is None else src, buf.at[s], beside_send, recv_sem.at[19 + row], beside)

    def spread(row, src=None):
        s = slot(rows[row], b)
        full(s, 3 + 3 * row, device(0, 1), src)
        full(s, 4 + 3 * row, device(0, 3), src)
        share(s, row, src)

    def start_first():
        s = slot(a, b)
        full(s, 0, device(1, 0), own)
        full(s, 1, device(3, 0), own)

    def start_second():
        spread(0, own)

    def first_before():
        s = slot(rows[1], b)
        arrived(s, 0)
        half(s, 0, 2, device(1, 0))
        spread(1)

    def first_after():
        s = slot(rows[2], b)
        arrived(s, 1)
        half(s, 1, 2, device(3, 0))
        spread(2)

    def first_across():
        arrived(slot(rows[3], b), 2)
        spread(3)

    def second(row):
        def step():
            s = slot(rows[row], before)
            arrived(s, 3 + 3 * row)
            half(s, 0, 5 + 3 * row, device(0, 1))
            share(s, row)
            s = slot(rows[row], after)
            arrived(s, 4 + 3 * row)
            half(s, 1, 5 + 3 * row, device(0, 3))
            share(s, row)

        return step

    def second_across(row):
        def step():
            s = slot(rows[row], across)
            arrived(s, 5 + 3 * row)
            share(s, row)

        return step

    steps = {
        "s": start_first,
        "t": start_second,
        "a": first_before,
        "b": first_after,
        "c": first_across,
        "r0": second(0),
        "r1": second(1),
        "r2": second(2),
        "r3": second(3),
        "x0": second_across(0),
        "x1": second_across(1),
        "x2": second_across(2),
        "x3": second_across(3),
    }

    def row_done(row):
        wait(buf.at[pl.ds(0, 4)], recv_sem.at[15 + row])

    def sent():
        wait(buf.at[pl.ds(0, 31)], send_sem)

    return steps, rows, row_done, sent


def kernel(
    tok_hbm,
    qw_hbm,
    kvw_hbm,
    ow_hbm,
    gain_hbm,
    cos_hbm,
    sin_hbm,
    qb_hbm,
    kvb_hbm,
    part_ref,
    cache_out,
    cache_ref,
    gain_ref,
    cos_ref,
    sin_ref,
    qb_ref,
    kvb_ref,
    tok,
    qw,
    kvw,
    kv,
    ow,
    oz,
    att,
    outp,
    qs,
    acc,
    kvacc,
    s_ref,
    m_ref,
    l_ref,
    o_ref,
    local_sem,
    ag_send,
    kvw_recv,
    qw_recv,
    kv_recv,
    cache_send,
    cache_recv,
    ow_send,
    oz_recv,
    ow_z,
    ow_y,
    ow_p,
    att_send,
    att_x,
    a2a_send,
    a2a_recv,
):
    c = lax.axis_index("ctx")
    r = lax.axis_index("rep")
    k = lax.rem(c, 2)
    y = lax.rem(lax.div(c, 2), 4)
    zh = lax.div(c, 8)
    x = lax.rem(r, 4)
    zl = lax.div(r, 4)
    where = (zh, y, k, r)
    c_pair = c - k

    def rep_peer(i):
        return lax.rem(r + i, REP)

    tok_copy = pltpu.make_async_copy(tok_hbm, tok, local_sem.at[0])
    tok_copy.start()
    kvw_own = pltpu.make_async_copy(kvw_hbm, kvw.at[c], local_sem.at[1])
    kvw_own.start()
    qw_own = pltpu.make_async_copy(qw_hbm, qw.at[c], local_sem.at[2])
    qw_own.start()

    small = []
    for i, (src, dst) in enumerate(
        (
            (gain_hbm, gain_ref),
            (cos_hbm, cos_ref),
            (sin_hbm, sin_ref),
            (qb_hbm, qb_ref),
            (kvb_hbm, kvb_ref),
        )
    ):
        small.append(pltpu.make_async_copy(src, dst, local_sem.at[4 + i]))
        small[-1].start()

    barrier = pltpu.get_barrier_semaphore()
    greet = [(c_pair + k, rep_peer(i)) for i in range(1, REP)]
    greet += [(c_pair + 1 - k, zl * 4 + lax.rem(x + i, 4)) for i in range(4)]
    greet += [(ctx_of(zh, lax.rem(y + d, 4), k), r) for d in (1, 3)]
    greet += [(ctx_of(lax.rem(zh + d, 4), y, k), r) for d in (1, 3)]
    for dev in greet:
        pl.semaphore_signal(barrier, inc=1, device_id=dev, device_id_type=MESH)
    pl.semaphore_wait(barrier, len(greet))

    kvw_steps, kvw_rows, kvw_row_done, kvw_sent = gather_steps(
        kvw, kvw_hbm, lambda s, i: kvw.at[s, pl.ds(128 * i, 128)], True, where, ag_send.at[0], kvw_recv
    )
    q_parts = []
    for i in range(2):
        view = qw.at[:, pl.ds(128 * i, 128)]
        q_parts.append(
            gather_steps(
                view,
                qw_hbm.at[pl.ds(128 * i, 128)],
                lambda s, j, i=i: qw.at[s, pl.ds(128 * i + 64 * j, 64)],
                True,
                where,
                ag_send.at[1 + 4 * i],
                qw_recv.at[i],
            )
        )
    q_rows = q_parts[0][1]
    side = lax.rem(r, 2)
    beside = (c, r + 1 - 2 * side)
    kv_mine, kv_other = kv.at[side], kv.at[1 - side]
    kv_steps, kv_rows, kv_row_done, kv_sent = gather_steps(
        kv_mine,
        None,
        lambda s, i: kv_mine.at[s, pl.ds(128 * i, 128)],
        True,
        where,
        ag_send.at[2],
        kv_recv,
        beside,
        ag_send.at[4],
    )

    def kv_relay(row):
        wait(kv_other.at[pl.ds(0, 4)], kv_recv.at[19 + row])
        for i in range(4):
            s = ctx_of(kv_rows[row], i, k)
            send(
                kv_other.at[s],
                kv_other.at[s],
                ag_send.at[3],
                kv_recv.at[23 + row],
                (ctx_of(zh, y, 1 - k), r),
            )

    z_next = (ctx_of(lax.rem(zh + 1, 4), y, k), r)
    z_last = (ctx_of(lax.rem(zh + 3, 4), y, k), r)
    y_next = (ctx_of(zh, lax.rem(y + 1, 4), k), r)
    y_last = (ctx_of(zh, lax.rem(y + 3, 4), k), r)
    partner = (ctx_of(zh, y, 1 - k), r)
    y_rows = (y, lax.rem(y + 3, 4), lax.rem(y + 1, 4), lax.rem(y + 2, 4))
    z_rows = (zh, lax.rem(zh + 3, 4), lax.rem(zh + 1, 4), lax.rem(zh + 2, 4))
    keeps = lax.rem(x, 2) == k

    def ow_place(y_, z_, first, count):
        cols = pl.ds(pl.multiple_of(128 * lax.rem(z_, 2), 128), 128)
        return ow.at[pl.ds(y_ * 8 + lax.div(z_, 2) * 4 + first, count), :, cols]

    def ow_pair(y_row, row):
        return ow_place(y_rows[y_row], z_rows[row], 2 * k, 2)

    def ow_half(y_row, row, i):
        return ow_place(y_rows[y_row], z_rows[row], 2 * k + i, 1)

    def oz_half(s, i):
        return oz.at[s, pl.ds(256 * i, 256)]

    def oz_start(i):
        rows = pl.ds(256 * i, 256)
        send(ow_hbm.at[rows], oz.at[zh, rows], ow_send.at[1], oz_recv.at[0], z_next)
        send(ow_hbm.at[rows], oz.at[zh, rows], ow_send.at[1], oz_recv.at[1], z_last)

    def oz_wait(row):
        s = z_rows[row]
        wait(oz.at[s], oz_recv.at[row - 1])
        if row == 1:
            send(oz_half(s, 0), oz_half(s, 0), ow_send.at[1], oz_recv.at[2], z_next)
        if row == 2:
            send(oz_half(s, 1), oz_half(s, 1), ow_send.at[1], oz_recv.at[2], z_last)

    def oz_give(row):
        z_ = z_rows[row]
        src = ow_hbm if row == 0 else oz.at[z_]
        spot = y * 8 + lax.div(z_, 2) * 4 + 2 * lax.rem(x, 2) + lax.div(x, 2)
        dst = ow.at[spot, :, pl.ds(pl.multiple_of(128 * lax.rem(z_, 2), 128), 128)]
        for j in range(2):
            worker = lax.rem(2 * k + j + z_, 4)
            part = src.at[:, pl.ds(128 * j, 128)]
            here = (worker == x) & keeps

            @pl.when(here)
            def _(part=part):
                pltpu.make_async_copy(part, dst, ow_z.at[row]).start()

            @pl.when(jnp.logical_not(here))
            def _(part=part, worker=worker):
                device = (ctx_of(zh, y, lax.rem(x, 2)), zl * 4 + worker)
                send(part, dst, ow_send.at[0], ow_z.at[row], device)

    def ow_y_start(i):
        part = ow_pair(0, i)
        wait(part, ow_z.at[i])
        send(part, part, ow_send.at[2], ow_y.at[i, 0], y_next)
        send(part, part, ow_send.at[2], ow_y.at[i, 1], y_last)
        send(part, part, ow_send.at[2], ow_p.at[0], partner)

    def ow_b(i):
        part, half = ow_pair(1, i), ow_half(1, i, 0)
        wait(part, ow_y.at[i, 0])
        send(half, half, ow_send.at[2], ow_y.at[i, 2], y_next)
        send(part, part, ow_send.at[2], ow_p.at[1], partner)
        part, half = ow_pair(2, i), ow_half(2, i, 1)
        wait(part, ow_y.at[i, 1])
        send(half, half, ow_send.at[2], ow_y.at[i, 2], y_last)
        send(part, part, ow_send.at[2], ow_p.at[2], partner)

    def ow_c(i):
        part = ow_pair(3, i)
        wait(part, ow_y.at[i, 2])
        send(part, part, ow_send.at[2], ow_p.at[3], partner)

    def ow_row_done(row):
        wait(ow.at[pl.ds(0, 4)], ow_p.at[row])

    def ow_sent():
        @pl.when(keeps)
        def _():
            wait(ow.at[pl.ds(0, 3)], ow_send.at[0])

        @pl.when(jnp.logical_not(keeps))
        def _():
            wait(ow.at[pl.ds(0, 4)], ow_send.at[0])

        wait(ow.at[pl.ds(0, 3)], ow_send.at[1])
        wait(ow.at[pl.ds(0, 28)], ow_send.at[2])

    def normalize(i, carry):
        rows = pl.ds(pl.multiple_of(i * 32, 32), 32)
        squares = jnp.zeros((32, 128), F32)
        for j in range(WIDTH // 128):
            v = tok[rows, j * 128 : (j + 1) * 128].astype(F32)
            squares = squares + v * v
        mean = jnp.sum(squares, axis=-1, keepdims=True) * (1.0 / WIDTH)
        scale = lax.rsqrt(mean + 1e-06)
        for j in range(WIDTH // 128):
            cols = slice(j * 128, (j + 1) * 128)
            v = tok[rows, cols].astype(F32)
            tok[rows, cols] = (v * scale * gain_ref[j : j + 1, :].astype(F32)).astype(BF16)
        return carry

    def norm(i):
        if i == 0:
            tok_copy.wait()
            for copy in small:
                copy.wait()
        lax.fori_loop(2 * i, 2 * i + 2, normalize, 0)

    my_block = cache_ref.at[:, pl.ds(pl.multiple_of(r * HEAD, HEAD), HEAD)]

    def kv_group(row):
        base = kvw_rows[row]
        if row == 0:
            kvw_own.wait()
            kvacc[...] = jnp.zeros_like(kvacc)
        kvw_row_done(row)

        def kv_product(i, carry):
            cols = pl.ds(pl.multiple_of(base * 2048 + i * 512, 512), 512)
            kvacc[...] += jnp.dot(
                tok[:, cols],
                kvw[pl.ds(base * 8 + 2 * i, 2)].reshape(512, HEAD),
                preferred_element_type=F32,
            )
            return carry

        lax.fori_loop(0, 4, kv_product, 0)

    side_head = side * KV_HEADS + lax.div(r, 2)
    first_peer = 2 * lax.rem(r, 4) + lax.div(r, 4)
    moves = first_peer != r
    all_peers = jnp.logical_not(moves)

    def cache_first():
        plain = kvacc[...] + kvb_ref[...].astype(F32)
        rotated = rotate(plain, cos_ref[...], sin_ref[...])
        my_block[...] = jnp.where(r < KV_HEADS, rotated, plain).astype(BF16)

        @pl.when(moves)
        def _():
            send(my_block, my_block, cache_send.at[0], cache_recv.at[0], (c, first_peer))

    def cache_wait():
        @pl.when(moves)
        def _():
            wait(kv_mine.at[0], cache_recv.at[0])

        column = pl.multiple_of(side_head * HEAD, HEAD)
        copy = pltpu.make_async_copy(
            cache_ref.at[:, pl.ds(column, HEAD)], kv_mine.at[c], local_sem.at[3]
        )
        copy.start()
        copy.wait()

    def cache_rest():
        for i in range(1, REP):

            @pl.when(rep_peer(i) != first_peer)
            def _():
                send(my_block, my_block, cache_send.at[1], cache_recv.at[1], (c, rep_peer(i)))

    def cache_done(sem):
        @pl.when(moves)
        def _():
            wait(kv_mine.at[pl.ds(0, 6)], sem)

        @pl.when(all_peers)
        def _():
            wait(kv_mine.at[pl.ds(0, 7)], sem)

    def q_group(row):
        base = q_rows[row]
        if row == 0:
            qw_own.wait()
            acc[...] = jnp.zeros_like(acc)
        for part in q_parts:
            part[2](row)

        def q_product(i, carry):
            cols = pl.ds(pl.multiple_of(base * 2048 + i * 512, 512), 512)
            acc[...] += jnp.dot(
                tok[:, cols],
                qw[pl.ds(base * 8 + 2 * i, 2)].reshape(512, LOCAL * HEAD),
                preferred_element_type=F32,
            )
            return carry

        lax.fori_loop(0, 4, q_product, 0)

    def q_finish():
        for h in range(LOCAL):
            v = acc[:, h * HEAD : (h + 1) * HEAD] + qb_ref[h : h + 1, :].astype(F32)
            qs[h] = rotate(v, cos_ref[...], sin_ref[...]).astype(BF16)

    def attend_row(row, heads):
        base = kv_rows[row]
        for h in heads:
            slot = h % 2
            peak = None
            for b in range(4):
                keys = kv[0, pl.ds(8 * base + 2 * b, 2)].reshape(512, HEAD)
                s = lax.dot_general(
                    qs[h], keys, (((1,), (1,)), ((), ())), preferred_element_type=F32
                )
                if row == 0:
                    key_pos = (4 * base + b) * 512 + lax.broadcasted_iota(jnp.int32, s.shape, 1)
                    query_pos = c * ROWS + lax.broadcasted_iota(jnp.int32, s.shape, 0)
                    s = jnp.where(key_pos <= query_pos, s, NEG)
                s_ref[slot, b] = s
                for t in range(4):
                    tile = s[:, t * 128 : (t + 1) * 128]
                    peak = tile if peak is None else jnp.maximum(peak, tile)
            m_new = jnp.broadcast_to(jnp.max(peak, axis=-1, keepdims=True), (ROWS, 128))
            if row == 0:
                total = jnp.zeros((ROWS, 128), F32)
                out = jnp.zeros((ROWS, HEAD), F32)
            else:
                m_old = m_ref[h]
                m_new = jnp.maximum(m_old, m_new)
                alpha = jnp.exp2((m_old - m_new) * EXP_SCALE)
                total = l_ref[h] * alpha
                out = o_ref[h] * alpha
            for b in range(4):
                values = kv[1, pl.ds(8 * base + 2 * b, 2)].reshape(512, HEAD)
                weights = []
                for t in range(4):
                    p = jnp.exp2((s_ref[slot, b, :, t * 128 : (t + 1) * 128] - m_new) * EXP_SCALE)
                    total = total + p
                    weights.append(p.astype(BF16))
                out = out + jnp.dot(
                    jnp.concatenate(weights, axis=1), values, preferred_element_type=F32
                )
            m_ref[h] = m_new
            l_ref[h] = total
            o_ref[h] = out

    def attend(row, pair):
        if pair == 0:
            kv_row_done(row)
            wait(kv_other.at[pl.ds(0, 4)], kv_recv.at[23 + row])
        heads = (2 * pair, 2 * pair + 1)
        if row == 0:
            attend_row(row, heads)
        else:
            pl.when(kv_rows[row] < zh)(functools.partial(attend_row, row, heads))

    x_next = (c, zl * 4 + lax.rem(x + 1, 4))
    x_last = (c, zl * 4 + lax.rem(x + 3, 4))

    def att_part(dx, h, half=None):
        rows = slice(None) if half is None else pl.ds(128 * half, 128)
        source = lax.rem(x + dx, 4)
        place = 2 * lax.rem(source, 2) + lax.div(source, 2)
        return att.at[rows, pl.ds(pl.multiple_of((place * LOCAL + h) * HEAD, HEAD), HEAD)]

    def att_share(h):
        part = att_part(0, h)
        total = jnp.sum(l_ref[h], axis=-1, keepdims=True)
        part[...] = (o_ref[h] / total).astype(BF16)
        send(part, part, att_send, att_x.at[h, 0], x_next)
        send(part, part, att_send, att_x.at[h, 1], x_last)

    def att_pass(h):
        wait(att_part(3, h), att_x.at[h, 0])
        half = att_part(3, h, 0)
        send(half, half, att_send, att_x.at[h, 2], x_next)
        wait(att_part(1, h), att_x.at[h, 1])
        half = att_part(1, h, 1)
        send(half, half, att_send, att_x.at[h, 2], x_last)

    def att_wait():
        for h in range(LOCAL):
            wait(att_part(2, h), att_x.at[h, 2])

    def own_part(row):
        src = outp.at[row, pl.ds(pl.multiple_of(r * 32, 32), 32)]
        return pltpu.make_async_copy(src, part_ref.at[r, y_rows[row]], local_sem.at[9 + row])

    cache_copy = pltpu.make_async_copy(cache_ref, cache_out, local_sem.at[13])

    def cache_finish():
        cache_done(cache_recv.at[1])
        cache_copy.start()

    def out_block(row):
        ow_row_done(row)
        y_ = y_rows[row]
        for i in range(2):
            rows = ow[pl.ds(y_ * 8 + 4 * i, 4)].reshape(4 * LOCAL * HEAD, 256)
            part = jnp.dot(att[...], rows, preferred_element_type=F32)
            outp[row, :, i * 256 : (i + 1) * 256] = part.astype(BF16)
        for i in range(1, REP):
            peer = rep_peer(i)
            src = outp.at[row, pl.ds(pl.multiple_of(peer * 32, 32), 32)]
            send(src, part_ref.at[r, y_], a2a_send, a2a_recv.at[row], (c, peer))
        own_part(row).start()

    ops = {"cs": cache_first,
        "cr": cache_rest,
        "cf": cache_finish,
        "cw": cache_wait, "qf": q_finish, "aw": att_wait}
    for prefix, steps in (
        ("k_", kvw_steps),
        ("q_", q_parts[0][0]),
        ("p_", q_parts[1][0]),
        ("v_", kv_steps),
    ):
        ops |= {prefix + name: step for name, step in steps.items()}
    for prefix, op in (
        ("n", norm),
        ("kg", kv_group),
        ("qg", q_group),
        ("oz", oz_wait),
        ("og", oz_give),
        ("vr", kv_relay),
        ("oy", ow_y_start),
        ("ob", ow_b),
        ("ox", ow_c),
        ("as", att_share),
        ("ap", att_pass),
        ("out", out_block),
    ):
        ops |= {prefix + str(i): functools.partial(op, i) for i in range(4)}
    for i in range(2):
        ops[f"ozs{i}"] = functools.partial(oz_start, i)
    for row in range(4):
        ops |= {f"at{row}{pair}": functools.partial(attend, row, pair) for pair in range(2)}
    for name in ORDER:
        ops[name]()

    for row in range(4):
        wait(outp.at[0, pl.ds(0, 224)], a2a_recv.at[row])

    kvw_sent()
    for part in q_parts:
        part[3]()
    kv_sent()
    ow_sent()
    wait(kv_mine.at[pl.ds(0, 16)], ag_send.at[3])
    wait(kv_mine.at[pl.ds(0, 16)], ag_send.at[4])
    cache_done(cache_send.at[1])
    cache_copy.wait()
    for row in range(4):
        own_part(row).wait()

    @pl.when(moves)
    def _():
        wait(kv_mine.at[0], cache_send.at[0])

    wait(att.at[:, pl.ds(0, 12 * HEAD)], att_send)
    wait(kv_mine.at[pl.ds(0, 14)], a2a_send)


def hand_over(part_in, cache_in, out_ref, cache_ref):
    for x in range(4):
        for zh in range(4):
            place = (x - zh) % 4
            for y in range(4):
                column = ctx_of(zh, y, place // 2) * 256 + place % 2 * 128
                cols = slice(zh * 128, (zh + 1) * 128)
                total = part_in[x, y, :, cols].astype(F32) + part_in[4 + x, y, :, cols].astype(F32)
                out_ref[:, column : column + 128] = total.astype(BF16)
    cache_ref[...] = cache_in[...]


def per_device(tokens, norm_gain, q_weight, q_bias, key_value_weight, kv_bias, out_weight):
    positions = lax.axis_index("ctx") * ROWS + jnp.arange(ROWS, dtype=jnp.int32)
    lane = jnp.arange(HEAD, dtype=jnp.int32)
    exponent = lax.rem(lane, HEAD // 2).astype(F32) * (2.0 / HEAD)
    inverse = ROPE_BASE ** (-exponent)
    angles = positions.astype(F32)[:, None] * inverse[None, :]
    cos = jnp.cos(angles)
    sin = jnp.where(lane[None, :] < HEAD // 2, -jnp.sin(angles), jnp.sin(angles))
    any_spec = pl.BlockSpec(memory_space=pl.ANY)
    vmem_spec = pl.BlockSpec(memory_space=pltpu.VMEM)
    dma = pltpu.SemaphoreType.DMA
    parts, cache = pl.pallas_call(
        kernel,
        out_shape=(
            jax.ShapeDtypeStruct((REP, 4, ROWS // REP, 512), BF16),
            jax.ShapeDtypeStruct((ROWS, 2 * KV_HEADS * HEAD), BF16),
        ),
        in_specs=[any_spec] * 9,
        out_specs=(any_spec, any_spec),
        scratch_shapes=[
            pltpu.VMEM((ROWS, 2 * KV_HEADS * HEAD), BF16),
            pltpu.VMEM((WIDTH // HEAD, HEAD), BF16),
            pltpu.VMEM((ROWS, HEAD), F32),
            pltpu.VMEM((ROWS, HEAD), F32),
            pltpu.VMEM((LOCAL, HEAD), BF16),
            pltpu.VMEM((1, HEAD), BF16),
            pltpu.VMEM((ROWS, WIDTH), BF16),
            pltpu.VMEM((CTX, 256, LOCAL * HEAD), BF16),
            pltpu.VMEM((CTX, 256, HEAD), BF16),
            pltpu.VMEM((2, CTX, ROWS, HEAD), BF16),
            pltpu.VMEM((CTX, LOCAL * HEAD, 256), BF16),
            pltpu.VMEM((4, LOCAL * HEAD, 256), BF16),
            pltpu.VMEM((ROWS, 4 * LOCAL * HEAD), BF16),
            pltpu.VMEM((4, ROWS, 512), BF16),
            pltpu.VMEM((LOCAL, ROWS, HEAD), BF16),
            pltpu.VMEM((ROWS, LOCAL * HEAD), F32),
            pltpu.VMEM((ROWS, HEAD), F32),
            pltpu.VMEM((2, 4, ROWS, 512), F32),
            pltpu.VMEM((LOCAL, ROWS, HEAD), F32),
            pltpu.VMEM((LOCAL, ROWS, HEAD), F32),
            pltpu.VMEM((LOCAL, ROWS, HEAD), F32),
            dma((14,)),
            dma((6,)),
            dma((19,)),
            dma((2, 19)),
            dma((27,)),
            dma((2,)),
            dma((2,)),
            dma((3,)),
            dma((3,)),
            dma((4,)),
            dma((4, 3)),
            dma((4,)),
            dma,
            dma((4, 3)),
            dma,
            dma((4,)),
        ],
        compiler_params=pltpu.CompilerParams(
            collective_id=0, has_side_effects=True, vmem_limit_bytes=60 << 20
        ),
    )(
        tokens,
        q_weight,
        key_value_weight,
        out_weight,
        norm_gain.reshape(WIDTH // HEAD, HEAD),
        cos,
        sin,
        q_bias.reshape(LOCAL, HEAD),
        kv_bias.reshape(1, HEAD),
    )
    return pl.pallas_call(
        hand_over,
        out_shape=(
            jax.ShapeDtypeStruct((ROWS // REP, WIDTH), BF16),
            jax.ShapeDtypeStruct(cache.shape, BF16),
        ),
        in_specs=[vmem_spec, vmem_spec],
        out_specs=(vmem_spec, vmem_spec),
    )(parts, cache)


def solution(mesh):
    in_specs = (
        P("ctx", None),
        P(),
        P("ctx", "rep"),
        P("rep"),
        P("ctx", "rep"),
        P("rep"),
        P("rep", "ctx"),
    )
    out_specs = (P(("ctx", "rep"), None), P("ctx", None))
    return jax.shard_map(
        per_device, mesh=mesh, in_specs=in_specs, out_specs=out_specs, check_vma=False
    )
```
